128 devices in a mesh: lat: 8 (over z_lo, x), lon: 16 (over z_hi, y, core).
Axes of the slice: x: 4, y: 4, z: 4 (z_hi: 2, z_lo: 2; z = z_hi * 2 + z_lo), core: 2. Of those that a mesh axis runs over, the one named last changes fastest.
Arguments:
- fields: bfloat16 [448, 896, 768], P('lat', 'lon'), may hold values from -6 to 6
- cotangent: bfloat16 [448, 896, 768], P('lat', 'lon'), may hold values from -6 to 6
- inner_weight: bfloat16 [8, 2, 96, 96], replicated, may hold values from -0.4375 to 0.4375
- outer_weight: bfloat16 [8, 2, 96, 96], replicated, may hold values from -0.4375 to 0.4375
Outputs:
- field_gradient: bfloat16 [448, 896, 768], P('lat', 'lon')
- inner_gradient: float32 [8, 2, 96, 96], replicated
- outer_gradient: float32 [8, 2, 96, 96], replicated
The draws below stay inside these ranges and needn't reach their ends.
All inputs are finite; a program needn't handle non-finite values.
Results may differ from the reference program's by a relative error of at most 0.012.
Values may be sent and summed in bfloat16 or wider, within the bound.
A program may use at most 128 MiB of HBM per device.

```python
import math
import jax
import jax.numpy as jnp

LATS = 448
LONS = 896
MODES = 128
WIDTH = 768
BLOCKS = 8
BLOCK_W = 96


def block_levels(own_key, extent, cuts, low, top_value):
    level, own = 1.0, jax.random.fold_in(own_key, 6)
    for axis_at, parts in cuts:
        draws = jnp.exp(jax.random.uniform(jax.random.fold_in(own, axis_at), (parts,), jnp.float32, low / len(cuts), top_value / len(cuts)))
        level = level * jnp.repeat(draws, extent[axis_at] // parts).reshape([-1 if axis == axis_at else 1 for axis in range(len(extent))])
    return level


def centred(key, extent, deviation, reach, split=(), kind=jnp.bfloat16):
    drawn = deviation * jax.random.normal(key, extent, jnp.float32)
    if split:
        drawn = drawn * block_levels(key, extent, split, -0.22, 0.18)
    return jnp.clip(drawn, -reach, reach).astype(kind)


def setup_inputs(seed: int = 0) -> dict:
    seeds = jax.random.split(jax.random.key(seed), 5)
    fields = centred(seeds[0], (LATS, LONS, WIDTH), 1.0, 6.0, ((0, 8), (1, 16)))
    cotangent = centred(seeds[1], (LATS, LONS, WIDTH), 1.0, 6.0, ((0, 8), (1, 16)))
    inner_weight = centred(seeds[2], (BLOCKS, 2, BLOCK_W, BLOCK_W), (2 * BLOCK_W) ** -0.5, 0.4375)
    outer_weight = centred(seeds[3], (BLOCKS, 2, BLOCK_W, BLOCK_W), (2 * BLOCK_W) ** -0.5, 0.4375)
    return dict(fields=fields, cotangent=cotangent, inner_weight=inner_weight, outer_weight=outer_weight)


def tables(row_total, col_total, period, row_first, col_first):
    row_ids = row_first + jnp.arange(row_total, dtype=jnp.int32)
    col_ids = col_first + jnp.arange(col_total, dtype=jnp.int32)
    phase = (row_ids[:, None] * col_ids[None, :] % period).astype(jnp.float32) * (2.0 * math.pi / period)
    factor = 1.0 / math.sqrt(period)
    return ((jnp.cos(phase) * factor).astype(jnp.bfloat16), (jnp.sin(phase) * factor).astype(jnp.bfloat16))

def gelu_pair(value):
    cdf = 0.5 * (1.0 + jax.scipy.special.erf(value * 0.7071067811865476))
    density = jnp.exp(-0.5 * value * value) * 0.3989422804014327
    return (value * cdf, cdf + value * density)

def widen(value):
    return value.astype(jnp.float32)

def complex_apply(left_r, left_i, weight):
    real_w = widen(weight[:, 0])
    imag_w = widen(weight[:, 1])
    real = jnp.einsum('pbi,bij->pbj', widen(left_r), real_w) - jnp.einsum('pbi,bij->pbj', widen(left_i), imag_w)
    imag = jnp.einsum('pbi,bij->pbj', widen(left_r), imag_w) + jnp.einsum('pbi,bij->pbj', widen(left_i), real_w)
    return (real, imag)

def complex_adjoint(adj_r, adj_i, weight):
    real_w = widen(weight[:, 0])
    imag_w = widen(weight[:, 1])
    real = jnp.einsum('pbj,bij->pbi', widen(adj_r), real_w) + jnp.einsum('pbj,bij->pbi', widen(adj_i), imag_w)
    imag = jnp.einsum('pbj,bij->pbi', widen(adj_i), real_w) - jnp.einsum('pbj,bij->pbi', widen(adj_r), imag_w)
    return (real, imag)

def complex_outer(left_r, left_i, adj_r, adj_i):
    real = jnp.einsum('pbi,pbj->bij', widen(left_r), widen(adj_r)) + jnp.einsum('pbi,pbj->bij', widen(left_i), widen(adj_i))
    imag = jnp.einsum('pbi,pbj->bij', widen(left_r), widen(adj_i)) - jnp.einsum('pbi,pbj->bij', widen(left_i), widen(adj_r))
    return jnp.stack([real, imag], axis=1)

def lat_forward(lat_cos, lat_sin, part_r, part_i):
    flat_r = part_r.reshape(LATS, -1)
    flat_i = part_i.reshape(LATS, -1)
    real = jnp.dot(lat_cos, flat_r, preferred_element_type=jnp.float32) + jnp.dot(lat_sin, flat_i, preferred_element_type=jnp.float32)
    imag = jnp.dot(lat_cos, flat_i, preferred_element_type=jnp.float32) - jnp.dot(lat_sin, flat_r, preferred_element_type=jnp.float32)
    return (real.astype(jnp.bfloat16).reshape(-1, BLOCKS, BLOCK_W), imag.astype(jnp.bfloat16).reshape(-1, BLOCKS, BLOCK_W))

def reference(fields, cotangent, inner_weight, outer_weight):
    lon_cos, lon_sin = tables(MODES, LONS, LONS, 0, 0)
    factor = jnp.where(jnp.arange(MODES) == 0, 1.0, 2.0).astype(jnp.bfloat16)[:, None]
    forward_table = jnp.concatenate([lon_cos, -lon_sin], axis=0)
    pull_table = jnp.concatenate([lon_cos * factor, -(lon_sin * factor)], axis=0)
    spectrum = jnp.einsum('kw,hwc->hkc', widen(forward_table), widen(fields)).astype(jnp.bfloat16)
    pulled = jnp.einsum('kw,hwc->hkc', widen(pull_table), widen(cotangent)).astype(jnp.bfloat16)
    lat_cos, lat_sin = tables(LATS, LATS, LATS, 0, 0)
    z_r, z_i = lat_forward(lat_cos, lat_sin, spectrum[:, :MODES], spectrum[:, MODES:])
    back_r, back_i = lat_forward(lat_cos, lat_sin, pulled[:, :MODES], pulled[:, MODES:])
    u_r, u_i = complex_apply(z_r, z_i, inner_weight)
    gelu_r, slope_r = gelu_pair(u_r)
    gelu_i, slope_i = gelu_pair(u_i)
    hidden_r = gelu_r.astype(jnp.bfloat16)
    hidden_i = gelu_i.astype(jnp.bfloat16)
    hidden_adj_r, hidden_adj_i = complex_adjoint(back_r, back_i, outer_weight)
    u_adj_r = (hidden_adj_r * slope_r).astype(jnp.bfloat16)
    u_adj_i = (hidden_adj_i * slope_i).astype(jnp.bfloat16)
    scale = 1.0 / math.sqrt(LATS * MODES)
    outer_gradient = complex_outer(hidden_r, hidden_i, back_r, back_i) * scale
    inner_gradient = complex_outer(z_r, z_i, u_adj_r, u_adj_i) * scale
    z_adj_r, z_adj_i = complex_adjoint(u_adj_r, u_adj_i, inner_weight)
    flat_r = z_adj_r.astype(jnp.bfloat16).reshape(LATS, -1)
    flat_i = z_adj_i.astype(jnp.bfloat16).reshape(LATS, -1)
    cos_back = lat_cos.T
    sin_back = lat_sin.T
    adj_r = jnp.dot(cos_back, flat_r, preferred_element_type=jnp.float32) - jnp.dot(sin_back, flat_i, preferred_element_type=jnp.float32)
    adj_i = jnp.dot(sin_back, flat_r, preferred_element_type=jnp.float32) + jnp.dot(cos_back, flat_i, preferred_element_type=jnp.float32)
    adj_r = adj_r.astype(jnp.bfloat16).reshape(LATS, MODES, WIDTH)
    adj_i = adj_i.astype(jnp.bfloat16).reshape(LATS, MODES, WIDTH)
    merged = jnp.concatenate([adj_r, adj_i], axis=1)
    field_gradient = jnp.einsum('hkc,kw->hwc', widen(merged), widen(forward_table)).astype(jnp.bfloat16)
    return (field_gradient, inner_gradient, outer_gradient)
```

```python
import functools
import math

import jax
import jax.numpy as jnp
import numpy as np
from jax import lax
from jax.experimental import pallas as pl
from jax.experimental.pallas import tpu as pltpu
from jax.sharding import PartitionSpec as P

LATS = 448
LONS = 896
MODES = 128
BLOCKS = 8
BLOCK_W = 96
MESH = pl.DeviceIdType.MESH
BF = jnp.bfloat16
F32 = jnp.float32


def trig(rows, cols, period):
    phase = (np.outer(rows, cols) % period) * (2.0 * np.pi / period)
    factor = 1.0 / math.sqrt(period)
    return np.cos(phase) * factor, np.sin(phase) * factor


def lon_rows(half):
    return half * 64 + np.arange(64)


def tables():
    forward = np.zeros((2, 2, 256, 448))
    inverse = np.zeros((2, 448, 256))
    for zh in range(2):
        cols = zh * 448 + np.arange(448)
        for place, half in enumerate((zh, 1 - zh)):
            ids = lon_rows(half)
            cos, sin = trig(ids, cols, LONS)
            both = np.stack([cos, -sin], axis=1).reshape(128, 448)
            weight = np.repeat(np.where(ids == 0, 1.0, 2.0), 2)[:, None]
            forward[0, zh, place * 128 : place * 128 + 128] = both
            forward[1, zh, place * 128 : place * 128 + 128] = both * weight
        for half in range(2):
            cos, sin = trig(lon_rows(half), cols, LONS)
            both = np.stack([cos, -sin], axis=1).reshape(128, 448)
            inverse[zh, :, half * 128 : half * 128 + 128] = both.T
    order = np.concatenate([np.arange(0, 448, 2), np.arange(1, 448, 2)])
    cos, sin = trig(np.arange(448), order, LATS)
    lat_forward = np.concatenate([cos, sin], axis=1)
    lat_inverse = np.concatenate([cos.T, sin.T], axis=1)
    place = np.zeros((2, 2, 256, 96))
    for parity in range(2):
        for j in range(192):
            channel = (j + 64 * parity) % 192
            place[parity, channel // 96, j, channel % 96] = 1.0
    cast = lambda a: jnp.asarray(a.astype(np.float32)).astype(BF)
    return tuple(cast(a) for a in (forward, lat_forward, lat_inverse, inverse, place))


def gelu_pair(value):
    cdf = 0.5 * (1.0 + lax.erf(value * 0.7071067811865476))
    density = jnp.exp(-0.5 * value * value) * 0.3989422804014327
    return value * cdf, cdf + value * density


def dot(a, b):
    return lax.dot_general(a, b, (((1,), (0,)), ((), ())), preferred_element_type=F32)


def dot_nt(a, b):
    return lax.dot_general(a, b, (((1,), (1,)), ((), ())), preferred_element_type=F32)


def dot_tn(a, b):
    return lax.dot_general(a, b, (((0,), (0,)), ((), ())), preferred_element_type=F32)


def low_half(shape):
    return lax.broadcasted_iota(jnp.int32, shape, len(shape) - 1) < 64


def swap_halves(first, second):
    low = low_half(first.shape)
    turned = pltpu.roll(jnp.where(low, second, first), 64, 1)
    return jnp.where(low, first, turned), jnp.where(low, turned, second)


def body(
    fields, cotangent, inner, outer, fwd, latf, latb, inv, place,
    out, grad,
    TS, PK, R, OWN, SND, ZR, SS, D, E, XB, ZB, HB, BB, UB, SL, AM, BM, W, SB, HR, GI, GO,
    tsem, raw_ss, rsem, z_ss, zsem, d_ss, dsem, w_ss, wsem, wz_ss, wzsem, o_ss, fsem, hsem, osem,
):
    lat = lax.axis_index("lat")
    lon = lax.axis_index("lon")
    zh = lon // 8
    s = lon % 8
    y = s // 2
    core = s % 2
    parity = y % 2
    d = 2 * lat + core
    my_tile = 3 * (y // 2) + 2 * parity
    zdev = (lat, (1 - zh) * 8 + s)

    def s_of(r):
        return (s + r) % 8

    def d_of(r):
        return (d + r) % 16

    def s_dev(s2):
        return (lat, zh * 8 + s2)

    def d_dev(d2):
        return (d2 // 2, zh * 8 + y * 2 + d2 % 2)

    def send(src, dst, send_sem, recv_sem, device):
        pltpu.make_async_remote_copy(
            src_ref=src, dst_ref=dst, send_sem=send_sem, recv_sem=recv_sem,
            device_id=device, device_id_type=MESH,
        ).start()

    def drain(ref, sem):
        pltpu.make_async_copy(ref, ref, sem).wait()

    sources = (fields, cotangent)
    for fc in range(2):
        for q in range(2):
            pltpu.make_async_copy(
                sources[fc].at[:, :, :, pl.ds(128 + 384 * q, 128)], TS.at[fc, :, :, q], tsem.at[fc]
            ).start()

    barrier = pltpu.get_barrier_semaphore()
    for r in range(1, 8):
        pl.semaphore_signal(barrier, inc=1, device_id=s_dev(s_of(r)), device_id_type=MESH)
    for r in range(1, 16):
        pl.semaphore_signal(barrier, inc=1, device_id=d_dev(d_of(r)), device_id_type=MESH)
    pl.semaphore_signal(barrier, inc=1, device_id=zdev, device_id_type=MESH)
    pl.semaphore_wait(barrier, 23)

    def issue(fc, jj):
        for kk in range(2):
            for i in range(2):
                g = 14 * kk + 2 * jj + i
                for q in range(2):
                    even, odd = swap_halves(
                        TS[fc, g, 0, q].astype(F32), TS[fc, g, 1, q].astype(F32)
                    )
                    PK[fc, g, 2 * q] = even.astype(BF)
                    PK[fc, g, 2 * q + 1] = odd.astype(BF)
        j = 7 * fc + jj
        for r in range(8):
            s2 = s_of(r)
            y2 = s2 // 2
            g0 = 14 * (s2 % 2) + 2 * jj
            lane = pl.multiple_of(128 * (3 * (y2 // 2) + 2 * (y2 % 2)), 128)
            pairs = (
                (sources[fc].at[pl.ds(g0, 2), :, :, pl.ds(lane, 128)], R.at[j, :, pl.ds(0, 2), s]),
                (PK.at[fc, pl.ds(g0, 2), y2], R.at[j, :, 2, s]),
            )
            for src, dst in pairs:
                if r == 0:
                    pltpu.make_async_copy(src, dst, rsem.at[j]).start()
                else:
                    send(src, dst, raw_ss, rsem.at[j], s_dev(s2))

    for fc in range(2):
        drain(TS.at[fc], tsem.at[fc])

        @pl.loop(0, 7)
        def _(jj, fc=fc):
            issue(fc, jj)

    for refs, target in ((inner, AM), (outer, BM)):
        for part in range(2):
            total = None
            for b in range(2):
                spot = place[parity, b]
                moved = dot_nt(dot(spot, refs[2 * y + b, part]).astype(BF), spot)
                total = moved if total is None else total + moved
            total = total.astype(BF)
            if part == 0:
                target[0:256, 0:256] = total
                target[256:512, 256:512] = total
            else:
                target[0:256, 256:512] = total
                target[256:512, 0:256] = -total

    def stage_b(t):
        fc = t // 7
        drain(R.at[t], rsem.at[t])
        table = fwd[fc, zh]
        for i in range(2):
            data = jnp.concatenate([R[t, i, u].reshape(448, 128) for u in range(3)], axis=1)
            part = dot(table, data)
            OWN[t % 2, i] = part[0:128]
            SND[t, i] = part[128:256].astype(BF)
        send(SND.at[t], ZR.at[t], z_ss, zsem.at[t], zdev)

    def stage_c(t):
        fc = t // 7
        jj = t % 7
        drain(ZR.at[t], zsem.at[t])
        for i in range(2):
            total = OWN[t % 2, i] + ZR[t, i].astype(F32)
            SS[t, i] = total.astype(BF).reshape(16, 8, 384)
        for r in range(16):
            d2 = d_of(r)
            src = SS.at[t, :, d2]
            dst = D.at[fc, d, pl.ds(2 * jj, 2)]
            if r == 0:
                pltpu.make_async_copy(src, dst, dsem.at[fc]).start()
            else:
                send(src, dst, d_ss, dsem.at[fc], d_dev(d2))

    def unpack(fc):
        drain(D.at[fc], dsem.at[fc])

        @pl.loop(0, 16)
        def _(dd):
            block = D[fc, dd].reshape(112, 384)
            for u in range(3):
                E[u, pl.ds(pl.multiple_of(112 * dd, 8), 112), :] = block[:, 128 * u : 128 * u + 128].astype(F32)

    def spread(m):
        for part in range(2):
            a, b, c = (E[u, pl.ds(2 * m + part, 224, stride=8), :] for u in range(3))
            turned = pltpu.roll(c, 64, 1)
            whole = jnp.concatenate(
                [jnp.concatenate([a, c], axis=1), jnp.concatenate([b, turned], axis=1)], axis=0
            )
            if part == 0:
                XB[0:448, 0:256] = whole.astype(BF)
                XB[448:896, 256:512] = (-whole).astype(BF)
            else:
                XB[0:448, 256:512] = whole.astype(BF)
                XB[448:896, 0:256] = whole.astype(BF)

    def fields_side():
        unpack(0)

        @pl.loop(0, 4)
        def _(m):
            spread(m)
            z = dot(latf[...], XB[...]).astype(BF)
            ZB[m] = z
            gelu, slope = gelu_pair(dot(z, AM[...]))
            HB[m] = gelu.astype(BF)
            SL[m] = slope

    @pl.loop(0, 10)
    def _(t):
        stage_b(t)

        @pl.when(t > 0)
        def _():
            stage_c(t - 1)

    fields_side()

    @pl.loop(10, 14)
    def _(t):
        stage_b(t)
        stage_c(t - 1)

    stage_c(13)
    unpack(1)

    @pl.loop(0, 4)
    def _(m):
        spread(m)
        back = dot(latf[...], XB[...]).astype(BF)
        BB[m] = back
        u_adj = (dot_nt(back, BM[...]) * SL[m]).astype(BF)
        UB[m] = u_adj
        z_adj = dot_nt(u_adj, AM[...])
        XB[0:448, :] = z_adj.astype(BF)
        XB[448:896, 0:256] = (-z_adj[:, 256:512]).astype(BF)
        XB[448:896, 256:512] = z_adj[:, 0:256].astype(BF)
        adj = dot(latb[...], XB[...])
        for part in range(2):
            own = adj[:, 256 * part : 256 * part + 256]
            c0 = own[0:224, 128:256]
            c1 = pltpu.roll(own[224:448, 128:256], 64, 1)
            rows = pl.ds(2 * m + part, 224, stride=8)
            E[0, rows, :] = own[0:224, 0:128]
            E[1, rows, :] = own[224:448, 0:128]
            E[2, rows, :] = jnp.where(low_half(c0.shape), c0, c1)

    @pl.loop(0, 16)
    def _(dd):
        for u in range(3):
            block = E[u, pl.ds(pl.multiple_of(112 * dd, 8), 112), :]
            SB[dd, :, :, 128 * u : 128 * u + 128] = block.reshape(14, 8, 128).astype(BF)

    for half in range(2):
        for r in range(16):
            d2 = d_of(r)
            src = SB.at[d2, pl.ds(7 * half, 7)]
            dst = W.at[pl.ds(7 * half, 7), zh * 16 + d]
            if r == 0:
                pltpu.make_async_copy(src, dst, wsem.at[half]).start()
            else:
                send(src, dst, w_ss, wsem.at[half], d_dev(d2))

    GI[...] = jnp.zeros_like(GI)
    GO[...] = jnp.zeros_like(GO)

    @pl.loop(0, 4)
    def _(m):
        GI[...] += dot_tn(ZB[m], UB[m])
        GO[...] += dot_tn(HB[m], BB[m])

    for kind, ref in enumerate((GI, GO)):
        for part in range(2):
            if part == 0:
                total = ref[0:256, 0:256] + ref[256:512, 256:512]
            else:
                total = ref[0:256, 256:512] - ref[256:512, 0:256]
            for b in range(2):
                spot = place[parity, b].astype(F32)
                rows = lax.dot_general(
                    spot, total, (((0,), (0,)), ((), ())),
                    precision=lax.Precision.HIGHEST, preferred_element_type=F32,
                )
                grad[2 * kind + part, b] = lax.dot_general(
                    rows, spot, (((1,), (0,)), ((), ())),
                    precision=lax.Precision.HIGHEST, preferred_element_type=F32,
                )

    for half in range(2):
        mine = W.at[pl.ds(7 * half, 7), pl.ds(16 * zh, 16)]
        drain(mine, wsem.at[half])
        send(mine, mine, wz_ss, wzsem.at[half], zdev)

    for half in range(2):
        drain(W.at[pl.ds(7 * half, 7), pl.ds(0, 16)], wzsem.at[half])

        @pl.loop(7 * half, 7 * half + 7)
        def _(g):
            piece = dot(inv[zh], W[g].reshape(256, 384)).astype(BF)
            for u in range(3):
                R[g, 0, u] = piece[:, 128 * u : 128 * u + 128].reshape(8, 56, 128)
            for r in range(8):
                s2 = s_of(r)
                lane = pl.multiple_of(128 * my_tile, 128)
                full = (R.at[g, 0, pl.ds(0, 2), s2], out.at[14 * core + g, :, :, pl.ds(lane, 128)])
                part = (R.at[g, 0, 2, s2], HR.at[y, core, g])
                if r == 0:
                    pltpu.make_async_copy(*full, fsem).start()
                    pltpu.make_async_copy(*part, hsem.at[g]).start()
                else:
                    send(*full, o_ss, fsem, s_dev(s2))
                    send(*part, o_ss, hsem.at[g], s_dev(s2))

    @pl.loop(0, 14)
    def _(g):
        drain(HR.at[:, :, g], hsem.at[g])
        for kk in range(2):
            for q in range(2):
                first, second = swap_halves(
                    HR[2 * q, kk, g].astype(F32), HR[2 * q + 1, kk, g].astype(F32)
                )
                TS[0, 14 * kk + g, 0, q] = first.astype(BF)
                TS[0, 14 * kk + g, 1, q] = second.astype(BF)

    for q in range(2):
        pltpu.make_async_copy(
            TS.at[0, :, :, q], out.at[:, :, :, pl.ds(128 + 384 * q, 128)], osem
        ).start()
    drain(TS.at[0], osem)
    drain(out.at[:, :, :, pl.ds(0, 512)], fsem)
    drain(R.at[:, :, :, pl.ds(0, 7)], raw_ss)
    drain(SND, z_ss)
    drain(SS.at[:, :, pl.ds(0, 15)], d_ss)
    drain(SB.at[pl.ds(0, 15)], w_ss)
    drain(W.at[:, pl.ds(0, 16)], wz_ss)
    drain(R.at[:, 0, :, pl.ds(0, 7)], o_ss)


def step(fields, cotangent, inner, outer):
    dma = pltpu.SemaphoreType.DMA
    anyspace = pl.BlockSpec(memory_space=pl.ANY)
    vmem = pl.BlockSpec(memory_space=pltpu.VMEM)
    scratch = [
        pltpu.VMEM((2, 28, 2, 2, 56, 128), BF),
        pltpu.VMEM((2, 28, 4, 56, 128), BF),
        pltpu.VMEM((14, 2, 3, 8, 56, 128), BF),
        pltpu.VMEM((2, 2, 128, 384), F32),
        pltpu.VMEM((14, 2, 128, 384), BF),
        pltpu.VMEM((14, 2, 128, 384), BF),
        pltpu.VMEM((14, 2, 16, 8, 384), BF),
        pltpu.VMEM((2, 16, 14, 8, 384), BF),
        pltpu.VMEM((3, 1792, 128), F32),
        pltpu.VMEM((896, 512), BF),
        pltpu.VMEM((4, 448, 512), BF),
        pltpu.VMEM((4, 448, 512), BF),
        pltpu.VMEM((4, 448, 512), BF),
        pltpu.VMEM((4, 448, 512), BF),
        pltpu.VMEM((4, 448, 512), F32),
        pltpu.VMEM((512, 512), BF),
        pltpu.VMEM((512, 512), BF),
        pltpu.VMEM((14, 32, 8, 384), BF),
        pltpu.VMEM((16, 14, 8, 384), BF),
        pltpu.VMEM((4, 2, 14, 56, 128), BF),
        pltpu.VMEM((512, 512), F32),
        pltpu.VMEM((512, 512), F32),
        dma((2,)), dma, dma((14,)), dma, dma((14,)), dma, dma((2,)), dma, dma((2,)),
        dma, dma((2,)), dma, dma, dma((14,)), dma,
    ]
    return pl.pallas_call(
        body,
        out_shape=(
            jax.ShapeDtypeStruct((28, 2, 56, 768), BF),
            jax.ShapeDtypeStruct((4, 2, 96, 96), F32),
        ),
        in_specs=[anyspace] * 2 + [vmem] * 7,
        out_specs=(anyspace, vmem),
        scratch_shapes=scratch,
        compiler_params=pltpu.CompilerParams(
            collective_id=0, has_side_effects=True, vmem_limit_bytes=67043328
        ),
        name="spectral_step",
    )(fields, cotangent, inner, outer, *tables())


def local(fields, cotangent, inner_weight, outer_weight):
    field_gradient, part = step(
        fields.reshape(28, 2, 56, 768),
        cotangent.reshape(28, 2, 56, 768),
        inner_weight,
        outer_weight,
    )
    y = lax.axis_index("lon") % 8 // 2
    part = part * (1.0 / math.sqrt(LATS * MODES))
    part = part.reshape(2, 2, 2, BLOCK_W, BLOCK_W).transpose(0, 2, 1, 3, 4)
    mine = jnp.where(jnp.arange(4)[None, :, None, None, None, None] == y, part[:, None], 0.0)
    total = lax.psum(mine.reshape(2, BLOCKS, 2, BLOCK_W, BLOCK_W), ("lat", "lon"))
    return field_gradient.reshape(fields.shape), total[0], total[1]


def solution(mesh):
    return jax.shard_map(
        local,
        mesh=mesh,
        in_specs=(P("lat", "lon", None), P("lat", "lon", None), P(), P()),
        out_specs=(P("lat", "lon", None), P(), P()),
        check_vma=False,
    )
```

```python
import math

import jax
import jax.numpy as jnp
import numpy as np
from jax import lax
from jax.experimental import pallas as pl
from jax.experimental.pallas import tpu as pltpu
from jax.sharding import PartitionSpec as P

LATS = 448
LONS = 896
MODES = 128
BLOCKS = 8
BLOCK_W = 96
MESH = pl.DeviceIdType.MESH
BF = jnp.bfloat16
F32 = jnp.float32


def trig(rows, cols, period):
    phase = (np.outer(rows, cols) % period) * (2.0 * np.pi / period)
    factor = 1.0 / math.sqrt(period)
    return np.cos(phase) * factor, np.sin(phase) * factor


def lon_rows(half):
    return half * 64 + np.arange(64)


def tables():
    forward = np.zeros((2, 256, 448))
    for zh in range(2):
        cols = zh * 448 + np.arange(448)
        for place, half in enumerate((zh, 1 - zh)):
            cos, sin = trig(lon_rows(half), cols, LONS)
            both = np.stack([cos, -sin], axis=1).reshape(128, 448)
            forward[zh, place * 128 : place * 128 + 128] = both
    order = np.concatenate([np.arange(0, 448, 2), np.arange(1, 448, 2)])
    cos, sin = trig(np.arange(448), order, LATS)
    lat_forward = np.concatenate([cos, sin], axis=1)
    cast = lambda a: jnp.asarray(a.astype(np.float32)).astype(BF)
    return cast(forward), cast(lat_forward)


def gelu_pair(value):
    cdf = 0.5 * (1.0 + lax.erf(value * 0.7071067811865476))
    density = jnp.exp(-0.5 * value * value) * 0.3989422804014327
    return value * cdf, cdf + value * density


def dot(a, b):
    return lax.dot_general(a, b, (((1,), (0,)), ((), ())), preferred_element_type=F32)


def dot_nt(a, b):
    return lax.dot_general(a, b, (((1,), (1,)), ((), ())), preferred_element_type=F32)


def dot_tn(a, b):
    return lax.dot_general(a, b, (((0,), (0,)), ((), ())), preferred_element_type=F32)


def low_half(shape):
    return lax.broadcasted_iota(jnp.int32, shape, len(shape) - 1) < 64


def swap_halves(first, second):
    low = low_half(first.shape)
    turned = pltpu.roll(jnp.where(low, second, first), 64, 1)
    return jnp.where(low, first, turned), jnp.where(low, turned, second)


def body(
    fields, cotangent, inner, outer, fwd, latf,
    out, inner_grad, outer_grad,
    TS, PK, R, OWN, SND, ZR, SS, D, E, XB, ZB, HB, BB, UB, SL, AM, BM, W, SB, HR, GI, GO,
    LB, IV, GL, GR, GS, GZ, GB, GA,
    tsem, raw_ss, rsem, z_ss, zsem, d_ss, dsem, w_ss, wsem, wz_ss, wzsem, o_ss, fsem, hsem, osem,
    g1s, g1r, g2s, g2r, g3s, g3r, g4s, g4r,
):
    lat = lax.axis_index("lat")
    lon = lax.axis_index("lon")
    zh = lon // 8
    s = lon % 8
    y = s // 2
    core = s % 2
    parity = y % 2
    d = 2 * lat + core
    my_tile = 3 * (y // 2) + 2 * parity
    zdev = (lat, (1 - zh) * 8 + s)

    def s_of(r):
        return (s + r) % 8

    def d_of(r):
        return (d + r) % 16

    def s_dev(s2):
        return (lat, zh * 8 + s2)

    def d_dev(d2):
        return (d2 // 2, zh * 8 + y * 2 + d2 % 2)

    def send(src, dst, send_sem, recv_sem, device):
        pltpu.make_async_remote_copy(
            src_ref=src, dst_ref=dst, send_sem=send_sem, recv_sem=recv_sem,
            device_id=device, device_id_type=MESH,
        ).start()

    def drain(ref, sem):
        pltpu.make_async_copy(ref, ref, sem).wait()

    sources = (fields, cotangent)
    for fc in range(2):
        for q in range(2):
            pltpu.make_async_copy(
                sources[fc].at[:, :, :, pl.ds(128 + 384 * q, 128)], TS.at[fc, :, :, q], tsem.at[fc]
            ).start()

    barrier = pltpu.get_barrier_semaphore()
    for r in range(1, 8):
        pl.semaphore_signal(barrier, inc=1, device_id=s_dev(s_of(r)), device_id_type=MESH)
    for r in range(1, 16):
        pl.semaphore_signal(barrier, inc=1, device_id=d_dev(d_of(r)), device_id_type=MESH)
    pl.semaphore_signal(barrier, inc=1, device_id=zdev, device_id_type=MESH)
    pl.semaphore_wait(barrier, 23)

    def issue(fc, jj):
        for kk in range(2):
            for i in range(2):
                g = 14 * kk + 2 * jj + i
                for q in range(2):
                    even, odd = swap_halves(
                        TS[fc, g, 0, q].astype(F32), TS[fc, g, 1, q].astype(F32)
                    )
                    PK[fc, g, 2 * q] = even.astype(BF)
                    PK[fc, g, 2 * q + 1] = odd.astype(BF)
        j = 7 * fc + jj
        for r in range(8):
            s2 = s_of(r)
            y2 = s2 // 2
            g0 = 14 * (s2 % 2) + 2 * jj
            lane = pl.multiple_of(128 * (3 * (y2 // 2) + 2 * (y2 % 2)), 128)
            pairs = (
                (sources[fc].at[pl.ds(g0, 2), :, :, pl.ds(lane, 128)], R.at[j, :, pl.ds(0, 2), s]),
                (PK.at[fc, pl.ds(g0, 2), y2], R.at[j, :, 2, s]),
            )
            for src, dst in pairs:
                if r == 0:
                    pltpu.make_async_copy(src, dst, rsem.at[j]).start()
                else:
                    send(src, dst, raw_ss, rsem.at[j], s_dev(s2))

    for fc in range(2):
        drain(TS.at[fc], tsem.at[fc])

        @pl.loop(0, 7)
        def _(jj, fc=fc):
            issue(fc, jj)

    def spot_of(b, width):
        rows = lax.broadcasted_iota(jnp.int32, (256, width), 0)
        cols = lax.broadcasted_iota(jnp.int32, (256, width), 1)
        hit = (lax.rem(rows + 64 * parity, 192) == 96 * b + cols) & (rows < 192) & (cols < 96)
        return jnp.where(hit, 1.0, 0.0).astype(F32)

    for part in range(2):
        LB[:, 448 * part : 448 * part + 448] = (
            latf[:, 448 * part : 448 * part + 448].astype(F32).T.astype(BF)
        )
    IV[...] = fwd[zh].astype(F32).T.astype(BF)

    for refs, target in ((inner, AM), (outer, BM)):
        for part in range(2):
            total = None
            for b in range(2):
                spot = spot_of(b, 96).astype(BF)
                moved = dot_nt(dot(spot, refs[2 * y + b, part]).astype(BF), spot)
                total = moved if total is None else total + moved
            total = total.astype(BF)
            if part == 0:
                target[0:256, 0:256] = total
                target[256:512, 256:512] = total
            else:
                target[0:256, 256:512] = total
                target[256:512, 0:256] = -total

    def stage_b(t):
        fc = t // 7
        drain(R.at[t], rsem.at[t])
        table = fwd[zh]
        ids = lax.broadcasted_iota(jnp.int32, (256, 384), 0)
        first = (ids < 2) & (zh == 0) | (ids >= 128) & (ids < 130) & (zh == 1)
        weight = jnp.where((fc == 0) | first, 1.0, 2.0)
        for i in range(2):
            data = jnp.concatenate([R[t, i, u].reshape(448, 128) for u in range(3)], axis=1)
            part = dot(table, data) * weight
            OWN[t % 2, i] = part[0:128]
            SND[t, i] = part[128:256].astype(BF)
        send(SND.at[t], ZR.at[t], z_ss, zsem.at[t], zdev)

    def stage_c(t):
        fc = t // 7
        jj = t % 7
        drain(ZR.at[t], zsem.at[t])
        for i in range(2):
            total = OWN[t % 2, i] + ZR[t, i].astype(F32)
            SS[t, i] = total.astype(BF).reshape(16, 8, 384)
        for r in range(16):
            d2 = d_of(r)
            src = SS.at[t, :, d2]
            dst = D.at[fc, d, pl.ds(2 * jj, 2)]
            if r == 0:
                pltpu.make_async_copy(src, dst, dsem.at[fc]).start()
            else:
                send(src, dst, d_ss, dsem.at[fc], d_dev(d2))

    def unpack(fc):
        drain(D.at[fc], dsem.at[fc])

        @pl.loop(0, 16)
        def _(dd):
            block = D[fc, dd].reshape(112, 384)
            for u in range(3):
                E[u, pl.ds(pl.multiple_of(112 * dd, 8), 112), :] = block[:, 128 * u : 128 * u + 128].astype(F32)

    def spread(m):
        for part in range(2):
            a, b, c = (E[u, pl.ds(2 * m + part, 224, stride=8), :] for u in range(3))
            turned = pltpu.roll(c, 64, 1)
            whole = jnp.concatenate(
                [jnp.concatenate([a, c], axis=1), jnp.concatenate([b, turned], axis=1)], axis=0
            )
            if part == 0:
                XB[0:448, 0:256] = whole.astype(BF)
                XB[448:896, 256:512] = (-whole).astype(BF)
            else:
                XB[0:448, 256:512] = whole.astype(BF)
                XB[448:896, 0:256] = whole.astype(BF)

    def fields_side():
        unpack(0)

        @pl.loop(0, 4)
        def _(m):
            spread(m)
            z = dot(latf[...], XB[...]).astype(BF)
            ZB[m] = z
            gelu, slope = gelu_pair(dot(z, AM[...]))
            HB[m] = gelu.astype(BF)
            SL[m] = slope

    @pl.loop(0, 10)
    def _(t):
        stage_b(t)

        @pl.when(t > 0)
        def _():
            stage_c(t - 1)

    fields_side()

    @pl.loop(10, 14)
    def _(t):
        stage_b(t)
        stage_c(t - 1)

    stage_c(13)
    unpack(1)

    @pl.loop(0, 4)
    def _(m):
        spread(m)
        back = dot(latf[...], XB[...]).astype(BF)
        BB[m] = back
        u_adj = (dot_nt(back, BM[...]) * SL[m]).astype(BF)
        UB[m] = u_adj
        z_adj = dot_nt(u_adj, AM[...])
        XB[0:448, :] = z_adj.astype(BF)
        XB[448:896, 0:256] = (-z_adj[:, 256:512]).astype(BF)
        XB[448:896, 256:512] = z_adj[:, 0:256].astype(BF)
        adj = dot(LB[...], XB[...])
        for part in range(2):
            own = adj[:, 256 * part : 256 * part + 256]
            c0 = own[0:224, 128:256]
            c1 = pltpu.roll(own[224:448, 128:256], 64, 1)
            rows = pl.ds(2 * m + part, 224, stride=8)
            E[0, rows, :] = own[0:224, 0:128]
            E[1, rows, :] = own[224:448, 0:128]
            E[2, rows, :] = jnp.where(low_half(c0.shape), c0, c1)

    @pl.loop(0, 16)
    def _(dd):
        for u in range(3):
            block = E[u, pl.ds(pl.multiple_of(112 * dd, 8), 112), :]
            SB[dd, :, :, 128 * u : 128 * u + 128] = block.reshape(14, 8, 128).astype(BF)

    for half in range(2):
        for r in range(16):
            d2 = d_of(r)
            src = SB.at[d2, pl.ds(7 * half, 7)]
            dst = W.at[pl.ds(7 * half, 7), d]
            if r == 0:
                pltpu.make_async_copy(src, dst, wsem.at[half]).start()
            else:
                send(src, dst, w_ss, wsem.at[half], d_dev(d2))

    GI[...] = jnp.zeros_like(GI)
    GO[...] = jnp.zeros_like(GO)

    @pl.loop(0, 4)
    def _(m):
        GI[...] += dot_tn(ZB[m], UB[m])
        GO[...] += dot_tn(HB[m], BB[m])

    for kind, ref in enumerate((GI, GO)):
        for part in range(2):
            if part == 0:
                total = ref[0:256, 0:256] + ref[256:512, 256:512]
            else:
                total = ref[0:256, 256:512] - ref[256:512, 0:256]
            for b in range(2):
                spot = spot_of(b, 128)
                rows = lax.dot_general(
                    spot, total, (((0,), (0,)), ((), ())),
                    precision=lax.Precision.HIGHEST, preferred_element_type=F32,
                )
                block = lax.dot_general(
                    rows, spot, (((1,), (0,)), ((), ())),
                    precision=lax.Precision.HIGHEST, preferred_element_type=F32,
                )
                at = 4 * (2 * kind + part) + 2 * b
                GL[at] = block[0:48]
                GL[at + 1] = block[48:96]

    for r in range(16):
        d2 = d_of(r)
        if r == 0:
            pltpu.make_async_copy(GL.at[d2], GR.at[d], g1r).start()
        else:
            send(GL.at[d2], GR.at[d], g1s, g1r, d_dev(d2))

    for half in range(2):
        mine = W.at[pl.ds(7 * half, 7), pl.ds(0, 16)]
        drain(mine, wsem.at[half])
        send(mine, W.at[pl.ds(7 * half, 7), pl.ds(16, 16)], wz_ss, wzsem.at[half], zdev)

    def stage_e(half):
        drain(W.at[pl.ds(7 * half, 7), pl.ds(0, 16)], wzsem.at[half])

        @pl.loop(7 * half, 7 * half + 7)
        def _(g):
            piece = dot(IV[...], W[g].reshape(256, 384)).astype(BF)
            for u in range(3):
                R[g, 0, u] = piece[:, 128 * u : 128 * u + 128].reshape(8, 56, 128)
            for r in range(8):
                s2 = s_of(r)
                lane = pl.multiple_of(128 * my_tile, 128)
                full = (R.at[g, 0, pl.ds(0, 2), s2], out.at[14 * core + g, :, :, pl.ds(lane, 128)])
                part = (R.at[g, 0, 2, s2], HR.at[y, core, g])
                if r == 0:
                    pltpu.make_async_copy(*full, fsem).start()
                    pltpu.make_async_copy(*part, hsem.at[g]).start()
                else:
                    send(*full, o_ss, fsem, s_dev(s2))
                    send(*part, o_ss, hsem.at[g], s_dev(s2))

    def finish(low, high):
        @pl.loop(low, high)
        def _(g):
            drain(HR.at[:, :, g], hsem.at[g])
            for kk in range(2):
                for q in range(2):
                    first, second = swap_halves(
                        HR[2 * q, kk, g].astype(F32), HR[2 * q + 1, kk, g].astype(F32)
                    )
                    TS[0, 14 * kk + g, 0, q] = first.astype(BF)
                    TS[0, 14 * kk + g, 1, q] = second.astype(BF)

    stage_e(0)
    drain(GR, g1r)
    GS[...] = jnp.sum(GR[...], axis=0)
    send(GS, GZ, g2s, g2r, zdev)
    stage_e(1)
    drain(GZ, g2r)
    GB[y] = ((GS[...] + GZ[...]) * (1.0 / math.sqrt(LATS * MODES))).astype(BF)
    for r in range(1, 4):
        send(GB.at[y], GB.at[y], g3s, g3r, s_dev((s + 2 * r) % 8))
    finish(0, 4)
    drain(GB.at[pl.ds(0, 3)], g3r)
    for r in range(16):
        d2 = d_of(r)
        if r == 0:
            pltpu.make_async_copy(GB, GA.at[d], g4r).start()
        else:
            send(GB, GA.at[d], g4s, g4r, d_dev(d2))
    finish(4, 14)
    drain(GA, g4r)
    for kind, ref in enumerate((inner_grad, outer_grad)):
        for part in range(2):
            for b in range(2):
                for h in range(2):
                    at = 4 * (2 * kind + part) + 2 * b + h
                    for y2 in range(4):
                        ref[2 * y2 + b, part, 48 * h : 48 * h + 48, :] = GA[at, y2].astype(F32)[:, 0:96]
    drain(GL.at[pl.ds(0, 15)], g1s)
    drain(GS, g2s)
    drain(GB.at[pl.ds(0, 3)], g3s)
    drain(GA.at[pl.ds(0, 15)], g4s)

    for q in range(2):
        pltpu.make_async_copy(
            TS.at[0, :, :, q], out.at[:, :, :, pl.ds(128 + 384 * q, 128)], osem
        ).start()
    drain(TS.at[0], osem)
    drain(out.at[:, :, :, pl.ds(0, 512)], fsem)
    drain(R.at[:, :, :, pl.ds(0, 7)], raw_ss)
    drain(SND, z_ss)
    drain(SS.at[:, :, pl.ds(0, 15)], d_ss)
    drain(SB.at[pl.ds(0, 15)], w_ss)
    drain(W.at[:, pl.ds(0, 16)], wz_ss)
    drain(R.at[:, 0, :, pl.ds(0, 7)], o_ss)


def step(fields, cotangent, inner, outer):
    dma = pltpu.SemaphoreType.DMA
    anyspace = pl.BlockSpec(memory_space=pl.ANY)
    vmem = pl.BlockSpec(memory_space=pltpu.VMEM)
    scratch = [
        pltpu.VMEM((2, 28, 2, 2, 56, 128), BF),
        pltpu.VMEM((2, 28, 4, 56, 128), BF),
        pltpu.VMEM((14, 2, 3, 8, 56, 128), BF),
        pltpu.VMEM((2, 2, 128, 384), F32),
        pltpu.VMEM((14, 2, 128, 384), BF),
        pltpu.VMEM((14, 2, 128, 384), BF),
        pltpu.VMEM((14, 2, 16, 8, 384), BF),
        pltpu.VMEM((2, 16, 14, 8, 384), BF),
        pltpu.VMEM((3, 1792, 128), F32),
        pltpu.VMEM((896, 512), BF),
        pltpu.VMEM((4, 448, 512), BF),
        pltpu.VMEM((4, 448, 512), BF),
        pltpu.VMEM((4, 448, 512), BF),
        pltpu.VMEM((4, 448, 512), BF),
        pltpu.VMEM((4, 448, 512), F32),
        pltpu.VMEM((512, 512), BF),
        pltpu.VMEM((512, 512), BF),
        pltpu.VMEM((14, 32, 8, 384), BF),
        pltpu.VMEM((16, 14, 8, 384), BF),
        pltpu.VMEM((4, 2, 14, 56, 128), BF),
        pltpu.VMEM((512, 512), F32),
        pltpu.VMEM((512, 512), F32),
        pltpu.VMEM((448, 896), BF),
        pltpu.VMEM((448, 256), BF),
        pltpu.VMEM((16, 48, 128), F32),
        pltpu.VMEM((16, 48, 128), F32),
        pltpu.VMEM((48, 128), F32),
        pltpu.VMEM((48, 128), F32),
        pltpu.VMEM((4, 48, 128), BF),
        pltpu.VMEM((16, 4, 48, 128), BF),
        dma((2,)), dma, dma((14,)), dma, dma((14,)), dma, dma((2,)), dma, dma((2,)),
        dma, dma((2,)), dma, dma, dma((14,)), dma,
        dma, dma, dma, dma, dma, dma, dma, dma,
    ]
    return pl.pallas_call(
        body,
        out_shape=(
            jax.ShapeDtypeStruct((28, 2, 56, 768), BF),
            jax.ShapeDtypeStruct((BLOCKS, 2, BLOCK_W, BLOCK_W), F32),
            jax.ShapeDtypeStruct((BLOCKS, 2, BLOCK_W, BLOCK_W), F32),
        ),
        in_specs=[anyspace] * 2 + [vmem] * 4,
        out_specs=(anyspace, vmem, vmem),
        scratch_shapes=scratch,
        compiler_params=pltpu.CompilerParams(
            collective_id=0, has_side_effects=True, vmem_limit_bytes=67043328
        ),
        name="spectral_step",
    )(fields, cotangent, inner, outer, *tables())


def local(fields, cotangent, inner_weight, outer_weight):
    field_gradient, inner_gradient, outer_gradient = step(
        fields.reshape(28, 2, 56, 768),
        cotangent.reshape(28, 2, 56, 768),
        inner_weight,
        outer_weight,
    )
    return field_gradient.reshape(fields.shape), inner_gradient, outer_gradient


def solution(mesh):
    return jax.shard_map(
        local,
        mesh=mesh,
        in_specs=(P("lat", "lon", None), P("lat", "lon", None), P(), P()),
        out_specs=(P("lat", "lon", None), P(), P()),
        check_vma=False,
    )
```

```python
import math

import jax
import jax.numpy as jnp
import numpy as np
from jax import lax
from jax.experimental import pallas as pl
from jax.experimental.pallas import tpu as pltpu
from jax.sharding import PartitionSpec as P

LATS = 448
LONS = 896
MODES = 128
BLOCKS = 8
BLOCK_W = 96
MESH = pl.DeviceIdType.MESH
AHEAD = 2
EARLY = 3
GRAD_AT = (0, 4, 6, 8, 11)
LAG = 1
BF = jnp.bfloat16
F32 = jnp.float32


def trig(rows, cols, period):
    phase = (np.outer(rows, cols) % period) * (2.0 * np.pi / period)
    factor = 1.0 / math.sqrt(period)
    return np.cos(phase) * factor, np.sin(phase) * factor


def lon_rows(half):
    return half * 64 + np.arange(64)


def tables():
    forward = np.zeros((2, 256, 448))
    for zh in range(2):
        cols = zh * 448 + np.arange(448)
        for place, half in enumerate((zh, 1 - zh)):
            cos, sin = trig(lon_rows(half), cols, LONS)
            both = np.stack([cos, -sin], axis=1).reshape(128, 448)
            forward[zh, place * 128 : place * 128 + 128] = both
    order = np.concatenate([np.arange(0, 448, 2), np.arange(1, 448, 2)])
    cos, sin = trig(np.arange(448), order, LATS)
    lat_forward = np.concatenate([cos, sin], axis=1)
    cast = lambda a: jnp.asarray(a.astype(np.float32)).astype(BF)
    return cast(forward), cast(lat_forward)


def gelu_pair(value):
    cdf = 0.5 * (1.0 + lax.erf(value * 0.7071067811865476))
    density = jnp.exp(-0.5 * value * value) * 0.3989422804014327
    return value * cdf, cdf + value * density


def dot(a, b):
    return lax.dot_general(a, b, (((1,), (0,)), ((), ())), preferred_element_type=F32)


def dot_nt(a, b):
    return lax.dot_general(a, b, (((1,), (1,)), ((), ())), preferred_element_type=F32)


def dot_tn(a, b):
    return lax.dot_general(a, b, (((0,), (0,)), ((), ())), preferred_element_type=F32)


def low_half(shape):
    return lax.broadcasted_iota(jnp.int32, shape, len(shape) - 1) < 64


def swap_halves(first, second):
    low = low_half(first.shape)
    turned = pltpu.roll(jnp.where(low, second, first), 64, 1)
    return jnp.where(low, first, turned), jnp.where(low, turned, second)


def body(
    fields, cotangent, inner_any, outer_any, fwd_any, latf_any,
    out, inner_grad, outer_grad,
    TS, PK, R, OWN, SND, ZR, SS, D, E, XB, ZB, HB, BB, UB, SL, AM, BM, W, SB, HR, GI, GO,
    LB, IV, GL, GR, GS, GZ, GB, GA, fwd, latf, inner, outer,
    tsem, raw_ss, rsem, z_ss, zsem, d_ss, dsem, w_ss, wsem, wz_ss, wzsem, o_ss, fsem, hsem, osem,
    g1s, g1r, g2s, g2r, g3s, g3r, g4s, g4r, psem,
):
    lat = lax.axis_index("lat")
    lon = lax.axis_index("lon")
    zh = lon // 8
    s = lon % 8
    y = s // 2
    core = s % 2
    parity = y % 2
    d = 2 * lat + core
    my_tile = 3 * (y // 2) + 2 * parity
    zdev = (lat, (1 - zh) * 8 + s)

    def s_of(r):
        return (s + r) % 8

    def d_of(r):
        return (d + r) % 16

    def s_dev(s2):
        return (lat, zh * 8 + s2)

    def d_dev(d2):
        return (d2 // 2, zh * 8 + y * 2 + d2 % 2)

    def send(src, dst, send_sem, recv_sem, device):
        pltpu.make_async_remote_copy(
            src_ref=src, dst_ref=dst, send_sem=send_sem, recv_sem=recv_sem,
            device_id=device, device_id_type=MESH,
        ).start()

    def drain(ref, sem):
        pltpu.make_async_copy(ref, ref, sem).wait()

    sources = (fields, cotangent)
    for fc in range(2):
        for q in range(2):
            pltpu.make_async_copy(
                sources[fc].at[:, :, :, pl.ds(128 + 384 * q, 128)], TS.at[fc, :, :, q], tsem.at[fc]
            ).start()

    loads = ((fwd_any, fwd), (latf_any, latf), (inner_any, inner), (outer_any, outer))
    for i, (src, dst) in enumerate(loads):
        pltpu.make_async_copy(src, dst, psem.at[i]).start()

    barrier = pltpu.get_barrier_semaphore()
    for r in range(1, 8):
        pl.semaphore_signal(barrier, inc=1, device_id=s_dev(s_of(r)), device_id_type=MESH)
    for r in range(1, 16):
        pl.semaphore_signal(barrier, inc=1, device_id=d_dev(d_of(r)), device_id_type=MESH)
    pl.semaphore_signal(barrier, inc=1, device_id=zdev, device_id_type=MESH)
    pl.semaphore_wait(barrier, 23)

    def pack(fc, jj):
        for kk in range(2):
            g = 14 * kk + jj
            for q in range(2):
                even, odd = swap_halves(TS[fc, g, 0, q].astype(F32), TS[fc, g, 1, q].astype(F32))
                PK[fc, g, 2 * q] = even.astype(BF)
                PK[fc, g, 2 * q + 1] = odd.astype(BF)

    def send_raw(fc, jj, full):
        j = 14 * fc + jj
        for r in range(8):
            s2 = s_of(r)
            y2 = s2 // 2
            g0 = 14 * (s2 % 2) + jj
            lane = pl.multiple_of(128 * (3 * (y2 // 2) + 2 * (y2 % 2)), 128)
            if full:
                src, dst = sources[fc].at[g0, :, :, pl.ds(lane, 128)], R.at[j, pl.ds(0, 2), s]
            else:
                src, dst = PK.at[fc, g0, y2], R.at[j, 2, s]
            if r == 0:
                pltpu.make_async_copy(src, dst, rsem.at[j]).start()
            else:
                send(src, dst, raw_ss, rsem.at[j], s_dev(s2))

    for fc in range(2):
        ahead = EARLY if fc == 0 else 0

        @pl.loop(0, ahead)
        def _(jj, fc=fc):
            send_raw(fc, jj, True)

        drain(TS.at[fc], tsem.at[fc])

        @pl.loop(0, 14)
        def _(jj, fc=fc, ahead=ahead):
            pack(fc, jj)
            send_raw(fc, jj, False)

            @pl.when(jj < 14 - ahead)
            def _():
                send_raw(fc, jj + ahead, True)

    def spot_of(b, width):
        rows = lax.broadcasted_iota(jnp.int32, (256, width), 0)
        cols = lax.broadcasted_iota(jnp.int32, (256, width), 1)
        hit = (lax.rem(rows + 64 * parity, 192) == 96 * b + cols) & (rows < 192) & (cols < 96)
        return jnp.where(hit, 1.0, 0.0).astype(F32)

    for i, (src, dst) in enumerate(loads):
        drain(dst, psem.at[i])
    for part in range(2):
        LB[:, 448 * part : 448 * part + 448] = (
            latf[:, 448 * part : 448 * part + 448].astype(F32).T.astype(BF)
        )
    IV[...] = fwd[zh].astype(F32).T.astype(BF)

    for refs, target in ((inner, AM), (outer, BM)):
        for part in range(2):
            total = None
            for b in range(2):
                spot = spot_of(b, 96).astype(BF)
                moved = dot_nt(dot(spot, refs[2 * y + b, part]).astype(BF), spot)
                total = moved if total is None else total + moved
            total = total.astype(BF)
            if part == 0:
                target[0:256, 0:256] = total
                target[256:512, 256:512] = total
            else:
                target[0:256, 256:512] = total
                target[256:512, 0:256] = -total

    def stage_b(t):
        fc = t // 14
        drain(R.at[t], rsem.at[t])
        ids = lax.broadcasted_iota(jnp.int32, (256, 384), 0)
        first = (ids < 2) & (zh == 0) | (ids >= 128) & (ids < 130) & (zh == 1)
        weight = jnp.where((fc == 0) | first, 1.0, 2.0)
        data = jnp.concatenate([R[t, u].reshape(448, 128) for u in range(3)], axis=1)
        part = dot(fwd[zh], data) * weight
        SND[t] = part[128:256].astype(BF)
        send(SND.at[t], ZR.at[t], z_ss, zsem.at[t], zdev)
        OWN[t % 2] = part[0:128]

    def stage_c(t):
        fc = t // 14
        jj = t % 14
        drain(ZR.at[t], zsem.at[t])
        total = OWN[t % 2] + ZR[t].astype(F32)
        SS[t] = total.astype(BF).reshape(16, 8, 384)
        for r in range(16):
            d2 = d_of(r)
            src = SS.at[t, d2]
            dst = D.at[fc, d, jj]
            if r == 0:
                pltpu.make_async_copy(src, dst, dsem.at[fc]).start()
            else:
                send(src, dst, d_ss, dsem.at[fc], d_dev(d2))

    def unpack(fc):
        drain(D.at[fc], dsem.at[fc])

        @pl.loop(0, 16)
        def _(dd):
            block = D[fc, dd].reshape(112, 384)
            for u in range(3):
                E[u, pl.ds(pl.multiple_of(112 * dd, 8), 112), :] = block[:, 128 * u : 128 * u + 128].astype(F32)

    def spread(m):
        for part in range(2):
            a, b, c = (E[u, pl.ds(2 * m + part, 224, stride=8), :] for u in range(3))
            turned = pltpu.roll(c, 64, 1)
            whole = jnp.concatenate(
                [jnp.concatenate([a, c], axis=1), jnp.concatenate([b, turned], axis=1)], axis=0
            )
            if part == 0:
                XB[0:448, 0:256] = whole.astype(BF)
                XB[448:896, 256:512] = (-whole).astype(BF)
            else:
                XB[0:448, 256:512] = whole.astype(BF)
                XB[448:896, 0:256] = whole.astype(BF)

    def fields_side(m):
        spread(m)
        z = dot(latf[...], XB[...]).astype(BF)
        ZB[m] = z
        gelu, slope = gelu_pair(dot(z, AM[...]))
        HB[m] = gelu.astype(BF)
        SL[m] = slope

    @pl.loop(0, 18)
    def _(t):
        stage_b(t)

        @pl.when(t > 0)
        def _():
            stage_c(t - 1)

    unpack(0)

    @pl.loop(0, 4)
    def _(m):
        @pl.loop(18 + 2 * m, 20 + 2 * m)
        def _(t):
            stage_b(t)
            stage_c(t - 1)

        fields_side(m)

    @pl.loop(26, 28)
    def _(t):
        stage_b(t)
        stage_c(t - 1)

    stage_c(27)
    unpack(1)

    @pl.loop(0, 4)
    def _(m):
        spread(m)
        back = dot(latf[...], XB[...]).astype(BF)
        BB[m] = back
        u_adj = (dot_nt(back, BM[...]) * SL[m]).astype(BF)
        UB[m] = u_adj
        z_adj = dot_nt(u_adj, AM[...])
        XB[0:448, :] = z_adj.astype(BF)
        XB[448:896, 0:256] = (-z_adj[:, 256:512]).astype(BF)
        XB[448:896, 256:512] = z_adj[:, 0:256].astype(BF)
        adj = dot(LB[...], XB[...])
        for part in range(2):
            own = adj[:, 256 * part : 256 * part + 256]
            c0 = own[0:224, 128:256]
            c1 = pltpu.roll(own[224:448, 128:256], 64, 1)
            rows = pl.ds(2 * m + part, 224, stride=8)
            E[0, rows, :] = own[0:224, 0:128]
            E[1, rows, :] = own[224:448, 0:128]
            E[2, rows, :] = jnp.where(low_half(c0.shape), c0, c1)

    def wsend(c):
        for dd in range(16):
            rows = pl.ds(pl.multiple_of(112 * dd + 8 * c, 8), 8)
            for u in range(3):
                SB[c, dd, :, 128 * u : 128 * u + 128] = E[u, rows, :].astype(BF)
        for r in range(16):
            d2 = d_of(r)
            src = SB.at[c, d2]
            dst = W.at[c, d]
            if r == 0:
                pltpu.make_async_copy(src, dst, wsem.at[c]).start()
            else:
                send(src, dst, w_ss, wsem.at[c], d_dev(d2))

    def relay(c):
        mine = W.at[c, pl.ds(0, 16)]
        drain(mine, wsem.at[c])
        send(mine, W.at[c, pl.ds(16, 16)], wz_ss, wzsem.at[c], zdev)

    def stage_e(g):
        drain(W.at[g, pl.ds(16, 16)], wzsem.at[g])
        piece = dot(IV[...], W[g].reshape(256, 384)).astype(BF)
        for u in range(3):
            R[g, u] = piece[:, 128 * u : 128 * u + 128].reshape(8, 56, 128)
        for r in range(8):
            s2 = s_of(r)
            lane = pl.multiple_of(128 * my_tile, 128)
            full = (R.at[g, pl.ds(0, 2), s2], out.at[14 * core + g, :, :, pl.ds(lane, 128)])
            part = (R.at[g, 2, s2], HR.at[y, core, g])
            if r == 0:
                pltpu.make_async_copy(*full, fsem).start()
                pltpu.make_async_copy(*part, hsem.at[g]).start()
            else:
                send(*full, o_ss, fsem, s_dev(s2))
                send(*part, o_ss, hsem.at[g], s_dev(s2))

    def weight_piece(kind, i, j):
        left = (ZB, HB)[kind][:, :, 256 * i : 256 * i + 256].reshape(1792, 256)
        right = (UB, BB)[kind][:, :, 256 * j : 256 * j + 256].reshape(1792, 256)
        (GI, GO)[kind][256 * i : 256 * i + 256, 256 * j : 256 * j + 256] = dot_tn(left, right)

    def collect():
        for kind, ref in enumerate((GI, GO)):
            for part in range(2):
                if part == 0:
                    total = ref[0:256, 0:256] + ref[256:512, 256:512]
                else:
                    total = ref[0:256, 256:512] - ref[256:512, 0:256]
                for b in range(2):
                    spot = spot_of(b, 128).astype(BF)
                    rows = dot_tn(spot, total.astype(BF)).astype(BF)
                    block = dot(rows, spot)
                    at = 4 * (2 * kind + part) + 2 * b
                    GL[at] = block[0:48]
                    GL[at + 1] = block[48:96]
        for r in range(16):
            d2 = d_of(r)
            if r == 0:
                pltpu.make_async_copy(GL.at[d2], GR.at[d], g1r).start()
            else:
                send(GL.at[d2], GR.at[d], g1s, g1r, d_dev(d2))

    def sum_rows():
        drain(GR, g1r)
        GS[...] = jnp.sum(GR[...], axis=0)
        send(GS, GZ, g2s, g2r, zdev)

    def sum_half():
        drain(GZ, g2r)
        GB[y] = ((GS[...] + GZ[...]) * (1.0 / math.sqrt(LATS * MODES))).astype(BF)
        for r in range(1, 4):
            send(GB.at[y], GB.at[y], g3s, g3r, s_dev((s + 2 * r) % 8))

    def spread_out():
        drain(GB.at[pl.ds(0, 3)], g3r)
        for r in range(16):
            d2 = d_of(r)
            if r == 0:
                pltpu.make_async_copy(GB, GA.at[d], g4r).start()
            else:
                send(GB, GA.at[d], g4s, g4r, d_dev(d2))

    for c in range(AHEAD):
        wsend(c)

    @pl.loop(0, 14)
    def _(c):
        @pl.when(c < 14 - AHEAD)
        def _():
            wsend(c + AHEAD)

        relay(c)

        @pl.when(c >= LAG)
        def _():
            stage_e(c - LAG)

        for i in range(8):
            @pl.when(c == GRAD_AT[0] + i // 2)
            def _(i=i):
                weight_piece(i // 4, i // 2 % 2, i % 2)

        for at, action in zip(GRAD_AT[1:], (collect, sum_rows, sum_half, spread_out)):
            pl.when(c == at)(action)

    def finish(low, high):
        @pl.loop(low, high)
        def _(g):
            drain(HR.at[:, :, g], hsem.at[g])
            for kk in range(2):
                for q in range(2):
                    first, second = swap_halves(
                        HR[2 * q, kk, g].astype(F32), HR[2 * q + 1, kk, g].astype(F32)
                    )
                    TS[0, 14 * kk + g, 0, q] = first.astype(BF)
                    TS[0, 14 * kk + g, 1, q] = second.astype(BF)

    @pl.loop(14 - LAG, 14)
    def _(g):
        stage_e(g)

    finish(0, 14)
    drain(GA, g4r)
    for kind, ref in enumerate((inner_grad, outer_grad)):
        for part in range(2):
            for b in range(2):
                for h in range(2):
                    at = 4 * (2 * kind + part) + 2 * b + h
                    for y2 in range(4):
                        ref[2 * y2 + b, part, 48 * h : 48 * h + 48, :] = GA[at, y2].astype(F32)[:, 0:96]
    drain(GL.at[pl.ds(0, 15)], g1s)
    drain(GS, g2s)
    drain(GB.at[pl.ds(0, 3)], g3s)
    drain(GA.at[pl.ds(0, 15)], g4s)

    for q in range(2):
        pltpu.make_async_copy(
            TS.at[0, :, :, q], out.at[:, :, :, pl.ds(128 + 384 * q, 128)], osem
        ).start()
    drain(TS.at[0], osem)
    drain(out.at[:, :, :, pl.ds(0, 512)], fsem)
    drain(R.at[:, :, pl.ds(0, 7)], raw_ss)
    drain(SND, z_ss)
    drain(SS.at[:, pl.ds(0, 15)], d_ss)
    drain(SB.at[:, pl.ds(0, 15)], w_ss)
    drain(W.at[:, pl.ds(0, 16)], wz_ss)
    drain(R.at[pl.ds(0, 14), :, pl.ds(0, 7)], o_ss)


def step(fields, cotangent, inner, outer):
    dma = pltpu.SemaphoreType.DMA
    anyspace = pl.BlockSpec(memory_space=pl.ANY)
    vmem = pl.BlockSpec(memory_space=pltpu.VMEM)
    scratch = [
        pltpu.VMEM((2, 28, 2, 2, 56, 128), BF),
        pltpu.VMEM((2, 28, 4, 56, 128), BF),
        pltpu.VMEM((28, 3, 8, 56, 128), BF),
        pltpu.VMEM((2, 128, 384), F32),
        pltpu.VMEM((28, 128, 384), BF),
        pltpu.VMEM((28, 128, 384), BF),
        pltpu.VMEM((28, 16, 8, 384), BF),
        pltpu.VMEM((2, 16, 14, 8, 384), BF),
        pltpu.VMEM((3, 1792, 128), F32),
        pltpu.VMEM((896, 512), BF),
        pltpu.VMEM((4, 448, 512), BF),
        pltpu.VMEM((4, 448, 512), BF),
        pltpu.VMEM((4, 448, 512), BF),
        pltpu.VMEM((4, 448, 512), BF),
        pltpu.VMEM((4, 448, 512), F32),
        pltpu.VMEM((512, 512), BF),
        pltpu.VMEM((512, 512), BF),
        pltpu.VMEM((14, 32, 8, 384), BF),
        pltpu.VMEM((14, 16, 8, 384), BF),
        pltpu.VMEM((4, 2, 14, 56, 128), BF),
        pltpu.VMEM((512, 512), F32),
        pltpu.VMEM((512, 512), F32),
        pltpu.VMEM((448, 896), BF),
        pltpu.VMEM((448, 256), BF),
        pltpu.VMEM((16, 48, 128), F32),
        pltpu.VMEM((16, 48, 128), F32),
        pltpu.VMEM((48, 128), F32),
        pltpu.VMEM((48, 128), F32),
        pltpu.VMEM((4, 48, 128), BF),
        pltpu.VMEM((16, 4, 48, 128), BF),
        pltpu.VMEM((2, 256, 448), BF),
        pltpu.VMEM((448, 896), BF),
        pltpu.VMEM((BLOCKS, 2, BLOCK_W, BLOCK_W), BF),
        pltpu.VMEM((BLOCKS, 2, BLOCK_W, BLOCK_W), BF),
        dma((2,)), dma, dma((28,)), dma, dma((28,)), dma, dma((2,)), dma, dma((14,)),
        dma, dma((14,)), dma, dma, dma((14,)), dma,
        dma, dma, dma, dma, dma, dma, dma, dma, dma((4,)),
    ]
    return pl.pallas_call(
        body,
        out_shape=(
            jax.ShapeDtypeStruct((28, 2, 56, 768), BF),
            jax.ShapeDtypeStruct((BLOCKS, 2, BLOCK_W, BLOCK_W), F32),
            jax.ShapeDtypeStruct((BLOCKS, 2, BLOCK_W, BLOCK_W), F32),
        ),
        in_specs=[anyspace] * 6,
        out_specs=(anyspace, vmem, vmem),
        scratch_shapes=scratch,
        compiler_params=pltpu.CompilerParams(
            collective_id=0, has_side_effects=True, vmem_limit_bytes=67043328
        ),
        name="spectral_step",
    )(fields, cotangent, inner, outer, *tables())


def local(fields, cotangent, inner_weight, outer_weight):
    field_gradient, inner_gradient, outer_gradient = step(
        fields.reshape(28, 2, 56, 768),
        cotangent.reshape(28, 2, 56, 768),
        inner_weight,
        outer_weight,
    )
    return field_gradient.reshape(fields.shape), inner_gradient, outer_gradient


def solution(mesh):
    return jax.shard_map(
        local,
        mesh=mesh,
        in_specs=(P("lat", "lon", None), P("lat", "lon", None), P(), P()),
        out_specs=(P("lat", "lon", None), P(), P()),
        check_vma=False,
    )
```

```python
import math

import jax
import jax.numpy as jnp
import numpy as np
from jax import lax
from jax.experimental import pallas as pl
from jax.experimental.pallas import tpu as pltpu
from jax.sharding import PartitionSpec as P

LATS = 448
LONS = 896
MODES = 128
BLOCKS = 8
BLOCK_W = 96
MESH = pl.DeviceIdType.MESH
AHEAD = 2
EARLY = 1
GRAD_AT = (0, 4, 6, 8, 10, 12)
LAG = 2
BF = jnp.bfloat16
F32 = jnp.float32


def trig(rows, cols, period):
    phase = (np.outer(rows, cols) % period) * (2.0 * np.pi / period)
    factor = 1.0 / math.sqrt(period)
    return np.cos(phase) * factor, np.sin(phase) * factor


def lon_rows(half):
    return half * 64 + np.arange(64)


def tables():
    forward = np.zeros((2, 256, 448))
    for zh in range(2):
        cols = zh * 448 + np.arange(448)
        for place, half in enumerate((zh, 1 - zh)):
            cos, sin = trig(lon_rows(half), cols, LONS)
            both = np.stack([cos, -sin], axis=1).reshape(128, 448)
            forward[zh, place * 128 : place * 128 + 128] = both
    order = np.concatenate([np.arange(0, 448, 2), np.arange(1, 448, 2)])
    cos, sin = trig(np.arange(448), order, LATS)
    lat_forward = np.concatenate([cos, sin], axis=1)
    cast = lambda a: jnp.asarray(a.astype(np.float32)).astype(BF)
    return cast(forward), cast(lat_forward)


def gelu_pair(value):
    cdf = 0.5 * (1.0 + lax.erf(value * 0.7071067811865476))
    density = jnp.exp(-0.5 * value * value) * 0.3989422804014327
    return value * cdf, cdf + value * density


def dot(a, b):
    return lax.dot_general(a, b, (((1,), (0,)), ((), ())), preferred_element_type=F32)


def dot_nt(a, b):
    return lax.dot_general(a, b, (((1,), (1,)), ((), ())), preferred_element_type=F32)


def dot_tn(a, b):
    return lax.dot_general(a, b, (((0,), (0,)), ((), ())), preferred_element_type=F32)


def low_half(shape):
    return lax.broadcasted_iota(jnp.int32, shape, len(shape) - 1) < 64


def swap_halves(first, second):
    low = low_half(first.shape)
    turned = pltpu.roll(jnp.where(low, second, first), 64, 1)
    return jnp.where(low, first, turned), jnp.where(low, turned, second)


def body(
    fields, cotangent, inner_any, outer_any, fwd_any, latf_any,
    out, inner_grad, outer_grad,
    TS, PK, R, OWN, SND, ZR, SS, D, E, XB, ZB, HB, BB, UB, SL, AM, BM, W, SB, HR, GI, GO,
    LB, IV, GL, GR, GS, GT, GY, GZ, GB, GA, fwd, latf, inner, outer,
    tsem, raw_ss, rsem, z_ss, zsem, d_ss, dsem, w_ss, wsem, wz_ss, wzsem, o_ss, fsem, hsem, osem,
    g1s, g1r, g2s, g2r, g5s, g5r, g3s, g3r, g4s, g4r, psem,
):
    lat = lax.axis_index("lat")
    lon = lax.axis_index("lon")
    zh = lon // 8
    s = lon % 8
    y = s // 2
    core = s % 2
    parity = y % 2
    d = 2 * lat + core
    my_tile = 3 * (y // 2) + 2 * parity
    zdev = (lat, (1 - zh) * 8 + s)
    x = lat % 4
    zl = lat // 4
    own = 2 * x + core
    ldev = ((1 - zl) * 4 + x, lon)

    def s_of(r):
        return (s + r) % 8

    def d_of(r):
        return (d + r) % 16

    def o_of(r):
        return (own + r) % 8

    def o_dev(o2):
        return (zl * 4 + o2 // 2, zh * 8 + y * 2 + o2 % 2)

    def s_dev(s2):
        return (lat, zh * 8 + s2)

    def d_dev(d2):
        return (d2 // 2, zh * 8 + y * 2 + d2 % 2)

    def send(src, dst, send_sem, recv_sem, device):
        pltpu.make_async_remote_copy(
            src_ref=src, dst_ref=dst, send_sem=send_sem, recv_sem=recv_sem,
            device_id=device, device_id_type=MESH,
        ).start()

    def drain(ref, sem):
        pltpu.make_async_copy(ref, ref, sem).wait()

    sources = (fields, cotangent)
    for fc in range(2):
        for q in range(2):
            pltpu.make_async_copy(
                sources[fc].at[:, :, :, pl.ds(128 + 384 * q, 128)], TS.at[fc, :, :, q], tsem.at[fc]
            ).start()

    loads = ((fwd_any, fwd), (latf_any, latf), (inner_any, inner), (outer_any, outer))
    for i, (src, dst) in enumerate(loads):
        pltpu.make_async_copy(src, dst, psem.at[i]).start()

    barrier = pltpu.get_barrier_semaphore()
    for r in range(1, 8):
        pl.semaphore_signal(barrier, inc=1, device_id=s_dev(s_of(r)), device_id_type=MESH)
    for r in range(1, 16):
        pl.semaphore_signal(barrier, inc=1, device_id=d_dev(d_of(r)), device_id_type=MESH)
    pl.semaphore_signal(barrier, inc=1, device_id=zdev, device_id_type=MESH)
    pl.semaphore_wait(barrier, 23)

    def pack(fc, jj):
        for kk in range(2):
            g = 14 * kk + jj
            for q in range(2):
                even, odd = swap_halves(TS[fc, g, 0, q].astype(F32), TS[fc, g, 1, q].astype(F32))
                PK[fc, g, 2 * q] = even.astype(BF)
                PK[fc, g, 2 * q + 1] = odd.astype(BF)

    def send_raw(fc, jj, full):
        j = 14 * fc + jj
        for r in range(8):
            s2 = s_of(r)
            y2 = s2 // 2
            g0 = 14 * (s2 % 2) + jj
            lane = pl.multiple_of(128 * (3 * (y2 // 2) + 2 * (y2 % 2)), 128)
            if full:
                src, dst = sources[fc].at[g0, :, :, pl.ds(lane, 128)], R.at[j, pl.ds(0, 2), s]
            else:
                src, dst = PK.at[fc, g0, y2], R.at[j, 2, s]
            if r == 0:
                pltpu.make_async_copy(src, dst, rsem.at[j]).start()
            else:
                send(src, dst, raw_ss, rsem.at[j], s_dev(s2))

    for fc in range(2):
        ahead = EARLY if fc == 0 else 0

        @pl.loop(0, ahead)
        def _(jj, fc=fc):
            send_raw(fc, jj, True)

        drain(TS.at[fc], tsem.at[fc])

        @pl.loop(0, 14)
        def _(jj, fc=fc, ahead=ahead):
            pack(fc, jj)
            send_raw(fc, jj, False)

            @pl.when(jj < 14 - ahead)
            def _():
                send_raw(fc, jj + ahead, True)

    def spot_of(b, width):
        rows = lax.broadcasted_iota(jnp.int32, (256, width), 0)
        cols = lax.broadcasted_iota(jnp.int32, (256, width), 1)
        hit = (lax.rem(rows + 64 * parity, 192) == 96 * b + cols) & (rows < 192) & (cols < 96)
        return jnp.where(hit, 1.0, 0.0).astype(F32)

    for i, (src, dst) in enumerate(loads):
        drain(dst, psem.at[i])
    for part in range(2):
        LB[:, 448 * part : 448 * part + 448] = (
            latf[:, 448 * part : 448 * part + 448].astype(F32).T.astype(BF)
        )
    IV[...] = fwd[zh].astype(F32).T.astype(BF)

    for refs, target in ((inner, AM), (outer, BM)):
        for part in range(2):
            total = None
            for b in range(2):
                spot = spot_of(b, 96).astype(BF)
                moved = dot_nt(dot(spot, refs[2 * y + b, part]).astype(BF), spot)
                total = moved if total is None else total + moved
            total = total.astype(BF)
            if part == 0:
                target[0:256, 0:256] = total
                target[256:512, 256:512] = total
            else:
                target[0:256, 256:512] = total
                target[256:512, 0:256] = -total

    def stage_b(t):
        fc = t // 14
        drain(R.at[t], rsem.at[t])
        ids = lax.broadcasted_iota(jnp.int32, (256, 384), 0)
        first = (ids < 2) & (zh == 0) | (ids >= 128) & (ids < 130) & (zh == 1)
        weight = jnp.where((fc == 0) | first, 1.0, 2.0)
        data = jnp.concatenate([R[t, u].reshape(448, 128) for u in range(3)], axis=1)
        part = dot(fwd[zh], data) * weight
        SND[t] = part[128:256].astype(BF)
        send(SND.at[t], ZR.at[t], z_ss, zsem.at[t], zdev)
        OWN[t % 2] = part[0:128]

    def stage_c(t):
        fc = t // 14
        jj = t % 14
        drain(ZR.at[t], zsem.at[t])
        total = OWN[t % 2] + ZR[t].astype(F32)
        SS[t] = total.astype(BF).reshape(16, 8, 384)
        for r in range(16):
            d2 = d_of(r)
            src = SS.at[t, d2]
            dst = D.at[fc, d, jj]
            if r == 0:
                pltpu.make_async_copy(src, dst, dsem.at[fc]).start()
            else:
                send(src, dst, d_ss, dsem.at[fc], d_dev(d2))

    def unpack(fc):
        drain(D.at[fc], dsem.at[fc])

        @pl.loop(0, 16)
        def _(dd):
            block = D[fc, dd].reshape(112, 384)
            for u in range(3):
                E[u, pl.ds(pl.multiple_of(112 * dd, 8), 112), :] = block[:, 128 * u : 128 * u + 128].astype(F32)

    def spread(m):
        for part in range(2):
            a, b, c = (E[u, pl.ds(2 * m + part, 224, stride=8), :] for u in range(3))
            turned = pltpu.roll(c, 64, 1)
            whole = jnp.concatenate(
                [jnp.concatenate([a, c], axis=1), jnp.concatenate([b, turned], axis=1)], axis=0
            )
            if part == 0:
                XB[0:448, 0:256] = whole.astype(BF)
                XB[448:896, 256:512] = (-whole).astype(BF)
            else:
                XB[0:448, 256:512] = whole.astype(BF)
                XB[448:896, 0:256] = whole.astype(BF)

    def fields_side(m):
        spread(m)
        z = dot(latf[...], XB[...]).astype(BF)
        ZB[m] = z
        gelu, slope = gelu_pair(dot(z, AM[...]))
        HB[m] = gelu.astype(BF)
        SL[m] = slope

    @pl.loop(0, 18)
    def _(t):
        stage_b(t)

        @pl.when(t > 0)
        def _():
            stage_c(t - 1)

    unpack(0)

    @pl.loop(0, 4)
    def _(m):
        @pl.loop(18 + 2 * m, 20 + 2 * m)
        def _(t):
            stage_b(t)
            stage_c(t - 1)

        fields_side(m)

    @pl.loop(26, 28)
    def _(t):
        stage_b(t)
        stage_c(t - 1)

    stage_c(27)
    unpack(1)

    @pl.loop(0, 4)
    def _(m):
        spread(m)
        back = dot(latf[...], XB[...]).astype(BF)
        BB[m] = back
        u_adj = (dot_nt(back, BM[...]) * SL[m]).astype(BF)
        UB[m] = u_adj
        z_adj = dot_nt(u_adj, AM[...])
        XB[0:448, :] = z_adj.astype(BF)
        XB[448:896, 0:256] = (-z_adj[:, 256:512]).astype(BF)
        XB[448:896, 256:512] = z_adj[:, 0:256].astype(BF)
        adj = dot(LB[...], XB[...])
        for part in range(2):
            own = adj[:, 256 * part : 256 * part + 256]
            c0 = own[0:224, 128:256]
            c1 = pltpu.roll(own[224:448, 128:256], 64, 1)
            rows = pl.ds(2 * m + part, 224, stride=8)
            E[0, rows, :] = own[0:224, 0:128]
            E[1, rows, :] = own[224:448, 0:128]
            E[2, rows, :] = jnp.where(low_half(c0.shape), c0, c1)

    def wsend(c):
        for dd in range(16):
            rows = pl.ds(pl.multiple_of(112 * dd + 8 * c, 8), 8)
            for u in range(3):
                SB[c, dd, :, 128 * u : 128 * u + 128] = E[u, rows, :].astype(BF)
        for r in range(16):
            d2 = d_of(r)
            src = SB.at[c, d2]
            dst = W.at[c, d]
            if r == 0:
                pltpu.make_async_copy(src, dst, wsem.at[c]).start()
            else:
                send(src, dst, w_ss, wsem.at[c], d_dev(d2))

    def relay(c):
        mine = W.at[c, pl.ds(0, 16)]
        drain(mine, wsem.at[c])
        send(mine, W.at[c, pl.ds(16, 16)], wz_ss, wzsem.at[c], zdev)

    def stage_e(g):
        drain(W.at[g, pl.ds(16, 16)], wzsem.at[g])
        piece = dot(IV[...], W[g].reshape(256, 384)).astype(BF)
        for u in range(3):
            R[g, u] = piece[:, 128 * u : 128 * u + 128].reshape(8, 56, 128)
        for r in range(8):
            s2 = s_of(r)
            lane = pl.multiple_of(128 * my_tile, 128)
            full = (R.at[g, pl.ds(0, 2), s2], out.at[14 * core + g, :, :, pl.ds(lane, 128)])
            part = (R.at[g, 2, s2], HR.at[y, core, g])
            if r == 0:
                pltpu.make_async_copy(*full, fsem).start()
                pltpu.make_async_copy(*part, hsem.at[g]).start()
            else:
                send(*full, o_ss, fsem, s_dev(s2))
                send(*part, o_ss, hsem.at[g], s_dev(s2))

    def weight_piece(kind, i, j):
        left = (ZB, HB)[kind][:, :, 256 * i : 256 * i + 256].reshape(1792, 256)
        right = (UB, BB)[kind][:, :, 256 * j : 256 * j + 256].reshape(1792, 256)
        (GI, GO)[kind][256 * i : 256 * i + 256, 256 * j : 256 * j + 256] = dot_tn(left, right)

    def collect():
        for kind, ref in enumerate((GI, GO)):
            for part in range(2):
                if part == 0:
                    total = ref[0:256, 0:256] + ref[256:512, 256:512]
                else:
                    total = ref[0:256, 256:512] - ref[256:512, 0:256]
                for b in range(2):
                    spot = spot_of(b, 128).astype(BF)
                    rows = dot_tn(spot, total.astype(BF)).astype(BF)
                    block = dot(rows, spot)
                    GL[2 * (2 * kind + part) + b] = block[0:96].astype(BF)
        for r in range(8):
            o2 = o_of(r)
            if r == 0:
                pltpu.make_async_copy(GL.at[o2], GR.at[own], g1r).start()
            else:
                send(GL.at[o2], GR.at[own], g1s, g1r, o_dev(o2))

    def sum_rows():
        drain(GR, g1r)
        GS[...] = jnp.sum(GR[...].astype(F32), axis=0)
        send(GS, GY, g2s, g2r, ldev)

    def sum_near():
        drain(GY, g2r)
        GT[...] = GS[...] + GY[...]
        send(GT, GZ, g5s, g5r, zdev)

    def sum_far():
        drain(GZ, g5r)
        GB[y] = ((GT[...] + GZ[...]) * (1.0 / math.sqrt(LATS * MODES))).astype(BF)
        for r in range(1, 4):
            send(GB.at[y], GB.at[y], g3s, g3r, s_dev((s + 2 * r) % 8))

    def spread_out():
        drain(GB.at[pl.ds(0, 3)], g3r)
        for r in range(8):
            o2 = o_of(r)
            if r == 0:
                pltpu.make_async_copy(GB, GA.at[own], g4r).start()
            else:
                send(GB, GA.at[own], g4s, g4r, o_dev(o2))

    for c in range(AHEAD):
        wsend(c)

    @pl.loop(0, 14)
    def _(c):
        @pl.when(c < 14 - AHEAD)
        def _():
            wsend(c + AHEAD)

        relay(c)

        @pl.when(c >= LAG)
        def _():
            stage_e(c - LAG)

        for i in range(8):
            @pl.when(c == GRAD_AT[0] + i // 2)
            def _(i=i):
                weight_piece(i // 4, i // 2 % 2, i % 2)

        for at, action in zip(GRAD_AT[1:], (collect, sum_rows, sum_near, sum_far, spread_out)):
            pl.when(c == at)(action)

    def finish(low, high):
        @pl.loop(low, high)
        def _(g):
            drain(HR.at[:, :, g], hsem.at[g])
            for kk in range(2):
                for q in range(2):
                    first, second = swap_halves(
                        HR[2 * q, kk, g].astype(F32), HR[2 * q + 1, kk, g].astype(F32)
                    )
                    TS[0, 14 * kk + g, 0, q] = first.astype(BF)
                    TS[0, 14 * kk + g, 1, q] = second.astype(BF)
                    pltpu.make_async_copy(
                        TS.at[0, 14 * kk + g, :, q],
                        out.at[14 * kk + g, :, :, pl.ds(128 + 384 * q, 128)], osem,
                    ).start()

    @pl.loop(14 - LAG, 14)
    def _(g):
        stage_e(g)

    finish(0, 14)
    drain(GA, g4r)
    for kind, ref in enumerate((inner_grad, outer_grad)):
        for part in range(2):
            for b in range(2):
                at = 2 * (2 * kind + part) + b
                for y2 in range(4):
                    ref[2 * y2 + b, part] = GA[at, y2].astype(F32)[:, 0:96]
    drain(GL.at[pl.ds(0, 7)], g1s)
    drain(GS, g2s)
    drain(GT, g5s)
    drain(GB.at[pl.ds(0, 3)], g3s)
    drain(GA.at[pl.ds(0, 7)], g4s)

    drain(TS.at[0], osem)
    drain(out.at[:, :, :, pl.ds(0, 512)], fsem)
    drain(R.at[:, :, pl.ds(0, 7)], raw_ss)
    drain(SND, z_ss)
    drain(SS.at[:, pl.ds(0, 15)], d_ss)
    drain(SB.at[:, pl.ds(0, 15)], w_ss)
    drain(W.at[:, pl.ds(0, 16)], wz_ss)
    drain(R.at[pl.ds(0, 14), :, pl.ds(0, 7)], o_ss)


def step(fields, cotangent, inner, outer):
    dma = pltpu.SemaphoreType.DMA
    anyspace = pl.BlockSpec(memory_space=pl.ANY)
    vmem = pl.BlockSpec(memory_space=pltpu.VMEM)
    scratch = [
        pltpu.VMEM((2, 28, 2, 2, 56, 128), BF),
        pltpu.VMEM((2, 28, 4, 56, 128), BF),
        pltpu.VMEM((28, 3, 8, 56, 128), BF),
        pltpu.VMEM((2, 128, 384), F32),
        pltpu.VMEM((28, 128, 384), BF),
        pltpu.VMEM((28, 128, 384), BF),
        pltpu.VMEM((28, 16, 8, 384), BF),
        pltpu.VMEM((2, 16, 14, 8, 384), BF),
        pltpu.VMEM((3, 1792, 128), F32),
        pltpu.VMEM((896, 512), BF),
        pltpu.VMEM((4, 448, 512), BF),
        pltpu.VMEM((4, 448, 512), BF),
        pltpu.VMEM((4, 448, 512), BF),
        pltpu.VMEM((4, 448, 512), BF),
        pltpu.VMEM((4, 448, 512), F32),
        pltpu.VMEM((512, 512), BF),
        pltpu.VMEM((512, 512), BF),
        pltpu.VMEM((14, 32, 8, 384), BF),
        pltpu.VMEM((14, 16, 8, 384), BF),
        pltpu.VMEM((4, 2, 14, 56, 128), BF),
        pltpu.VMEM((512, 512), F32),
        pltpu.VMEM((512, 512), F32),
        pltpu.VMEM((448, 896), BF),
        pltpu.VMEM((448, 256), BF),
        pltpu.VMEM((8, 96, 128), BF),
        pltpu.VMEM((8, 96, 128), BF),
        pltpu.VMEM((96, 128), F32),
        pltpu.VMEM((96, 128), F32),
        pltpu.VMEM((96, 128), F32),
        pltpu.VMEM((96, 128), F32),
        pltpu.VMEM((4, 96, 128), BF),
        pltpu.VMEM((8, 4, 96, 128), BF),
        pltpu.VMEM((2, 256, 448), BF),
        pltpu.VMEM((448, 896), BF),
        pltpu.VMEM((BLOCKS, 2, BLOCK_W, BLOCK_W), BF),
        pltpu.VMEM((BLOCKS, 2, BLOCK_W, BLOCK_W), BF),
        dma((2,)), dma, dma((28,)), dma, dma((28,)), dma, dma((2,)), dma, dma((14,)),
        dma, dma((14,)), dma, dma, dma((14,)), dma,
        dma, dma, dma, dma, dma, dma, dma, dma, dma, dma, dma((4,)),
    ]
    return pl.pallas_call(
        body,
        out_shape=(
            jax.ShapeDtypeStruct((28, 2, 56, 768), BF),
            jax.ShapeDtypeStruct((BLOCKS, 2, BLOCK_W, BLOCK_W), F32),
            jax.ShapeDtypeStruct((BLOCKS, 2, BLOCK_W, BLOCK_W), F32),
        ),
        in_specs=[anyspace] * 6,
        out_specs=(anyspace, vmem, vmem),
        scratch_shapes=scratch,
        compiler_params=pltpu.CompilerParams(
            collective_id=0, has_side_effects=True, vmem_limit_bytes=67043328
        ),
        name="spectral_step",
    )(fields, cotangent, inner, outer, *tables())


def local(fields, cotangent, inner_weight, outer_weight):
    field_gradient, inner_gradient, outer_gradient = step(
        fields.reshape(28, 2, 56, 768),
        cotangent.reshape(28, 2, 56, 768),
        inner_weight,
        outer_weight,
    )
    return field_gradient.reshape(fields.shape), inner_gradient, outer_gradient


def solution(mesh):
    return jax.shard_map(
        local,
        mesh=mesh,
        in_specs=(P("lat", "lon", None), P("lat", "lon", None), P(), P()),
        out_specs=(P("lat", "lon", None), P(), P()),
        check_vma=False,
    )
```

```python
import math

import jax
import jax.numpy as jnp
import numpy as np
from jax import lax
from jax.experimental import pallas as pl
from jax.experimental.pallas import tpu as pltpu
from jax.sharding import PartitionSpec as P

LATS = 448
LONS = 896
MODES = 128
BLOCKS = 8
BLOCK_W = 96
MESH = pl.DeviceIdType.MESH
AHEAD = 2
EARLY = 1
GRAD_AT = (0, 4, 6, 8, 10, 12)
LAG = 2
BF = jnp.bfloat16
F32 = jnp.float32


def trig(rows, cols, period):
    phase = (np.outer(rows, cols) % period) * (2.0 * np.pi / period)
    factor = 1.0 / math.sqrt(period)
    return np.cos(phase) * factor, np.sin(phase) * factor


def lon_rows(half):
    return half * 64 + np.arange(64)


def tables():
    forward = np.zeros((2, 256, 448))
    for zh in range(2):
        cols = zh * 448 + np.arange(448)
        for place, half in enumerate((zh, 1 - zh)):
            cos, sin = trig(lon_rows(half), cols, LONS)
            both = np.stack([cos, -sin], axis=1).reshape(128, 448)
            forward[zh, place * 128 : place * 128 + 128] = both
    order = np.concatenate([np.arange(0, 448, 2), np.arange(1, 448, 2)])
    cos, sin = trig(np.arange(448), order, LATS)
    lat_forward = np.concatenate([cos, sin], axis=1)
    cast = lambda a: jnp.asarray(a.astype(np.float32)).astype(BF)
    return cast(forward), cast(lat_forward)


def gelu_pair(value):
    cdf = 0.5 * (1.0 + lax.erf(value * 0.7071067811865476))
    density = jnp.exp(-0.5 * value * value) * 0.3989422804014327
    return value * cdf, cdf + value * density


def dot(a, b):
    return lax.dot_general(a, b, (((1,), (0,)), ((), ())), preferred_element_type=F32)


def dot_nt(a, b):
    return lax.dot_general(a, b, (((1,), (1,)), ((), ())), preferred_element_type=F32)


def dot_tn(a, b):
    return lax.dot_general(a, b, (((0,), (0,)), ((), ())), preferred_element_type=F32)


def low_half(shape):
    return lax.broadcasted_iota(jnp.int32, shape, len(shape) - 1) < 64


def swap_halves(first, second):
    low = low_half(first.shape)
    turned = pltpu.roll(jnp.where(low, second, first), 64, 1)
    return jnp.where(low, first, turned), jnp.where(low, turned, second)


def body(
    fields, cotangent, inner_any, outer_any, fwd_any, latf_any,
    out, inner_grad, outer_grad,
    TS, PK, R, OWN, SND, ZR, SS, D, E, XB, ZB, HB, BB, UB, SL, AM, BM, W, SB, HR, GI, GO,
    LB, IV, GL, GR, GS, GT, GY, GZ, GB, GA, fwd, latf, inner, outer,
    tsem, raw_ss, rsem, z_ss, zsem, d_ss, dsem, w_ss, wsem, wz_ss, wzsem, o_ss, fsem, hsem, osem,
    g1s, g1r, g2s, g2r, g5s, g5r, g3s, g3r, g4s, g4r, psem,
):
    lat = lax.axis_index("lat")
    lon = lax.axis_index("lon")
    zh = lon // 8
    s = lon % 8
    y = s // 2
    core = s % 2
    parity = y % 2
    d = 2 * lat + core
    my_tile = 3 * (y // 2) + 2 * parity
    zdev = (lat, (1 - zh) * 8 + s)
    x = lat % 4
    zl = lat // 4
    own = 2 * x + core
    ldev = ((1 - zl) * 4 + x, lon)

    def s_of(r):
        return (s + r) % 8

    def d_of(r):
        return (d + r) % 16

    def o_of(r):
        return (own + r) % 8

    def o_dev(o2):
        return (zl * 4 + o2 // 2, zh * 8 + y * 2 + o2 % 2)

    def s_dev(s2):
        return (lat, zh * 8 + s2)

    def d_dev(d2):
        return (d2 // 2, zh * 8 + y * 2 + d2 % 2)

    def send(src, dst, send_sem, recv_sem, device):
        pltpu.make_async_remote_copy(
            src_ref=src, dst_ref=dst, send_sem=send_sem, recv_sem=recv_sem,
            device_id=device, device_id_type=MESH,
        ).start()

    def drain(ref, sem):
        pltpu.make_async_copy(ref, ref, sem).wait()

    sources = (fields, cotangent)
    for fc in range(2):
        for q in range(2):
            pltpu.make_async_copy(
                sources[fc].at[:, :, :, pl.ds(128 + 384 * q, 128)], TS.at[fc, :, :, q], tsem.at[fc]
            ).start()

    loads = ((fwd_any, fwd), (latf_any, latf), (inner_any, inner), (outer_any, outer))
    for i, (src, dst) in enumerate(loads):
        pltpu.make_async_copy(src, dst, psem.at[i]).start()

    barrier = pltpu.get_barrier_semaphore()
    for r in range(1, 8):
        pl.semaphore_signal(barrier, inc=1, device_id=s_dev(s_of(r)), device_id_type=MESH)
    for r in range(1, 16):
        pl.semaphore_signal(barrier, inc=1, device_id=d_dev(d_of(r)), device_id_type=MESH)
    pl.semaphore_signal(barrier, inc=1, device_id=zdev, device_id_type=MESH)
    pl.semaphore_wait(barrier, 23)

    def pack(fc, jj):
        for kk in range(2):
            g = 14 * kk + jj
            for q in range(2):
                even, odd = swap_halves(TS[fc, g, 0, q].astype(F32), TS[fc, g, 1, q].astype(F32))
                PK[fc, g, 2 * q] = even.astype(BF)
                PK[fc, g, 2 * q + 1] = odd.astype(BF)

    def send_raw(fc, jj, full):
        j = 14 * fc + jj
        for r in range(8):
            s2 = s_of(r)
            y2 = s2 // 2
            g0 = 14 * (s2 % 2) + jj
            lane = pl.multiple_of(128 * (3 * (y2 // 2) + 2 * (y2 % 2)), 128)
            if full:
                src, dst = sources[fc].at[g0, :, :, pl.ds(lane, 128)], R.at[j, pl.ds(0, 2), s]
            else:
                src, dst = PK.at[fc, g0, y2], R.at[j, 2, s]
            if r == 0:
                pltpu.make_async_copy(src, dst, rsem.at[j]).start()
            else:
                send(src, dst, raw_ss, rsem.at[j], s_dev(s2))

    for fc in range(2):
        ahead = EARLY if fc == 0 else 0

        @pl.loop(0, ahead)
        def _(jj, fc=fc):
            send_raw(fc, jj, True)

        drain(TS.at[fc], tsem.at[fc])

        @pl.loop(0, 14)
        def _(jj, fc=fc, ahead=ahead):
            pack(fc, jj)
            send_raw(fc, jj, False)

            @pl.when(jj < 14 - ahead)
            def _():
                send_raw(fc, jj + ahead, True)

    def spot_of(b, width):
        rows = lax.broadcasted_iota(jnp.int32, (256, width), 0)
        cols = lax.broadcasted_iota(jnp.int32, (256, width), 1)
        hit = (lax.rem(rows + 64 * parity, 192) == 96 * b + cols) & (rows < 192) & (cols < 96)
        return jnp.where(hit, 1.0, 0.0).astype(F32)

    for i, (src, dst) in enumerate(loads):
        drain(dst, psem.at[i])
    for part in range(2):
        LB[:, 448 * part : 448 * part + 448] = (
            latf[:, 448 * part : 448 * part + 448].astype(F32).T.astype(BF)
        )
    IV[...] = fwd[zh].astype(F32).T.astype(BF)

    for refs, target in ((inner, AM), (outer, BM)):
        for part in range(2):
            total = None
            for b in range(2):
                spot = spot_of(b, 96).astype(BF)
                moved = dot_nt(dot(spot, refs[2 * y + b, part]).astype(BF), spot)
                total = moved if total is None else total + moved
            total = total.astype(BF)
            if part == 0:
                target[0:256, 0:256] = total
                target[256:512, 256:512] = total
            else:
                target[0:256, 256:512] = total
                target[256:512, 0:256] = -total

    def stage_b(t):
        fc = t // 14
        drain(R.at[t], rsem.at[t])
        ids = lax.broadcasted_iota(jnp.int32, (256, 384), 0)
        first = (ids < 2) & (zh == 0) | (ids >= 128) & (ids < 130) & (zh == 1)
        weight = jnp.where((fc == 0) | first, 1.0, 2.0)
        data = jnp.concatenate([R[t, u].reshape(448, 128) for u in range(3)], axis=1)
        part = dot(fwd[zh], data) * weight
        SND[t] = part[128:256].astype(BF)
        send(SND.at[t], ZR.at[t], z_ss, zsem.at[t], zdev)
        OWN[t % 2] = part[0:128]

    def stage_c(t):
        fc = t // 14
        jj = t % 14
        drain(ZR.at[t], zsem.at[t])
        total = OWN[t % 2] + ZR[t].astype(F32)
        SS[t] = total.astype(BF).reshape(16, 8, 384)
        for r in range(16):
            d2 = d_of(r)
            src = SS.at[t, d2]
            dst = D.at[fc, d, jj]
            if r == 0:
                pltpu.make_async_copy(src, dst, dsem.at[fc]).start()
            else:
                send(src, dst, d_ss, dsem.at[fc], d_dev(d2))

    def unpack(fc):
        drain(D.at[fc], dsem.at[fc])

        @pl.loop(0, 16)
        def _(dd):
            block = D[fc, dd].reshape(112, 384)
            for u in range(3):
                E[u, pl.ds(pl.multiple_of(112 * dd, 8), 112), :] = block[:, 128 * u : 128 * u + 128].astype(F32)

    def spread(m):
        for part in range(2):
            a, b, c = (E[u, pl.ds(2 * m + part, 224, stride=8), :] for u in range(3))
            turned = pltpu.roll(c, 64, 1)
            whole = jnp.concatenate(
                [jnp.concatenate([a, c], axis=1), jnp.concatenate([b, turned], axis=1)], axis=0
            )
            if part == 0:
                XB[0:448, 0:256] = whole.astype(BF)
                XB[448:896, 256:512] = (-whole).astype(BF)
            else:
                XB[0:448, 256:512] = whole.astype(BF)
                XB[448:896, 0:256] = whole.astype(BF)

    def fields_side(m):
        spread(m)
        z = dot(latf[...], XB[...]).astype(BF)
        ZB[m] = z
        gelu, slope = gelu_pair(dot(z, AM[...]))
        HB[m] = gelu.astype(BF)
        SL[m] = slope

    @pl.loop(0, 16)
    def _(t):
        stage_b(t)

        @pl.when(t > 0)
        def _():
            stage_c(t - 1)

    unpack(0)

    @pl.loop(0, 4)
    def _(m):
        @pl.loop(16 + 2 * m, 18 + 2 * m)
        def _(t):
            stage_b(t)
            stage_c(t - 1)

        fields_side(m)

    @pl.loop(24, 28)
    def _(t):
        stage_b(t)
        stage_c(t - 1)

    stage_c(27)
    unpack(1)

    @pl.loop(0, 4)
    def _(m):
        spread(m)
        back = dot(latf[...], XB[...]).astype(BF)
        BB[m] = back
        u_adj = (dot_nt(back, BM[...]) * SL[m]).astype(BF)
        UB[m] = u_adj
        z_adj = dot_nt(u_adj, AM[...])
        XB[0:448, :] = z_adj.astype(BF)
        XB[448:896, 0:256] = (-z_adj[:, 256:512]).astype(BF)
        XB[448:896, 256:512] = z_adj[:, 0:256].astype(BF)
        adj = dot(LB[...], XB[...])
        for part in range(2):
            own = adj[:, 256 * part : 256 * part + 256]
            c0 = own[0:224, 128:256]
            c1 = pltpu.roll(own[224:448, 128:256], 64, 1)
            rows = pl.ds(2 * m + part, 224, stride=8)
            E[0, rows, :] = own[0:224, 0:128]
            E[1, rows, :] = own[224:448, 0:128]
            E[2, rows, :] = jnp.where(low_half(c0.shape), c0, c1)

    def wsend(c):
        for dd in range(16):
            rows = pl.ds(pl.multiple_of(112 * dd + 8 * c, 8), 8)
            for u in range(3):
                SB[c, dd, :, 128 * u : 128 * u + 128] = E[u, rows, :].astype(BF)
        for r in range(16):
            d2 = d_of(r)
            src = SB.at[c, d2]
            dst = W.at[c, d]
            if r == 0:
                pltpu.make_async_copy(src, dst, wsem.at[c]).start()
            else:
                send(src, dst, w_ss, wsem.at[c], d_dev(d2))

    def relay(c):
        mine = W.at[c, pl.ds(0, 16)]
        drain(mine, wsem.at[c])
        send(mine, W.at[c, pl.ds(16, 16)], wz_ss, wzsem.at[c], zdev)

    def stage_e(g):
        drain(W.at[g, pl.ds(16, 16)], wzsem.at[g])
        piece = dot(IV[...], W[g].reshape(256, 384)).astype(BF)
        for u in range(3):
            R[g, u] = piece[:, 128 * u : 128 * u + 128].reshape(8, 56, 128)
        for r in range(8):
            s2 = s_of(r)
            lane = pl.multiple_of(128 * my_tile, 128)
            full = (R.at[g, pl.ds(0, 2), s2], out.at[14 * core + g, :, :, pl.ds(lane, 128)])
            part = (R.at[g, 2, s2], HR.at[y, core, g])
            if r == 0:
                pltpu.make_async_copy(*full, fsem).start()
                pltpu.make_async_copy(*part, hsem.at[g]).start()
            else:
                send(*full, o_ss, fsem, s_dev(s2))
                send(*part, o_ss, hsem.at[g], s_dev(s2))

    def weight_piece(kind, i, j):
        left = (ZB, HB)[kind][:, :, 256 * i : 256 * i + 256].reshape(1792, 256)
        right = (UB, BB)[kind][:, :, 256 * j : 256 * j + 256].reshape(1792, 256)
        (GI, GO)[kind][256 * i : 256 * i + 256, 256 * j : 256 * j + 256] = dot_tn(left, right)

    def collect():
        for kind, ref in enumerate((GI, GO)):
            for part in range(2):
                if part == 0:
                    total = ref[0:256, 0:256] + ref[256:512, 256:512]
                else:
                    total = ref[0:256, 256:512] - ref[256:512, 0:256]
                for b in range(2):
                    spot = spot_of(b, 128).astype(BF)
                    rows = dot_tn(spot, total.astype(BF)).astype(BF)
                    block = dot(rows, spot)
                    GL[2 * (2 * kind + part) + b] = block[0:96].astype(BF)
        for r in range(8):
            o2 = o_of(r)
            if r == 0:
                pltpu.make_async_copy(GL.at[o2], GR.at[own], g1r).start()
            else:
                send(GL.at[o2], GR.at[own], g1s, g1r, o_dev(o2))

    def sum_rows():
        drain(GR, g1r)
        GS[...] = jnp.sum(GR[...].astype(F32), axis=0)
        send(GS, GY, g2s, g2r, ldev)

    def sum_near():
        drain(GY, g2r)
        GT[...] = GS[...] + GY[...]
        send(GT, GZ, g5s, g5r, zdev)

    def sum_far():
        drain(GZ, g5r)
        GB[y] = ((GT[...] + GZ[...]) * (1.0 / math.sqrt(LATS * MODES))).astype(BF)
        for r in range(1, 4):
            send(GB.at[y], GB.at[y], g3s, g3r, s_dev((s + 2 * r) % 8))

    def spread_out():
        drain(GB.at[pl.ds(0, 3)], g3r)
        for r in range(8):
            o2 = o_of(r)
            if r == 0:
                pltpu.make_async_copy(GB, GA.at[own], g4r).start()
            else:
                send(GB, GA.at[own], g4s, g4r, o_dev(o2))

    for c in range(AHEAD):
        wsend(c)

    @pl.loop(0, 14)
    def _(c):
        @pl.when(c < 14 - AHEAD)
        def _():
            wsend(c + AHEAD)

        relay(c)

        @pl.when(c >= LAG)
        def _():
            stage_e(c - LAG)

        for i in range(8):
            @pl.when(c == GRAD_AT[0] + i // 2)
            def _(i=i):
                weight_piece(i // 4, i // 2 % 2, i % 2)

        for at, action in zip(GRAD_AT[1:], (collect, sum_rows, sum_near, sum_far, spread_out)):
            pl.when(c == at)(action)

    def finish(low, high):
        @pl.loop(low, high)
        def _(g):
            drain(HR.at[:, :, g], hsem.at[g])
            for kk in range(2):
                for q in range(2):
                    first, second = swap_halves(
                        HR[2 * q, kk, g].astype(F32), HR[2 * q + 1, kk, g].astype(F32)
                    )
                    TS[0, 14 * kk + g, 0, q] = first.astype(BF)
                    TS[0, 14 * kk + g, 1, q] = second.astype(BF)
                    pltpu.make_async_copy(
                        TS.at[0, 14 * kk + g, :, q],
                        out.at[14 * kk + g, :, :, pl.ds(128 + 384 * q, 128)], osem,
                    ).start()

    @pl.loop(14 - LAG, 14)
    def _(g):
        stage_e(g)

    finish(0, 14)
    drain(GA, g4r)
    for kind, ref in enumerate((inner_grad, outer_grad)):
        for part in range(2):
            for b in range(2):
                at = 2 * (2 * kind + part) + b
                for y2 in range(4):
                    ref[2 * y2 + b, part] = GA[at, y2].astype(F32)[:, 0:96]
    drain(GL.at[pl.ds(0, 7)], g1s)
    drain(GS, g2s)
    drain(GT, g5s)
    drain(GB.at[pl.ds(0, 3)], g3s)
    drain(GA.at[pl.ds(0, 7)], g4s)

    drain(TS.at[0], osem)
    drain(out.at[:, :, :, pl.ds(0, 512)], fsem)
    drain(R.at[:, :, pl.ds(0, 7)], raw_ss)
    drain(SND, z_ss)
    drain(SS.at[:, pl.ds(0, 15)], d_ss)
    drain(SB.at[:, pl.ds(0, 15)], w_ss)
    drain(W.at[:, pl.ds(0, 16)], wz_ss)
    drain(R.at[pl.ds(0, 14), :, pl.ds(0, 7)], o_ss)


def step(fields, cotangent, inner, outer):
    dma = pltpu.SemaphoreType.DMA
    anyspace = pl.BlockSpec(memory_space=pl.ANY)
    vmem = pl.BlockSpec(memory_space=pltpu.VMEM)
    scratch = [
        pltpu.VMEM((2, 28, 2, 2, 56, 128), BF),
        pltpu.VMEM((2, 28, 4, 56, 128), BF),
        pltpu.VMEM((28, 3, 8, 56, 128), BF),
        pltpu.VMEM((2, 128, 384), F32),
        pltpu.VMEM((28, 128, 384), BF),
        pltpu.VMEM((28, 128, 384), BF),
        pltpu.VMEM((28, 16, 8, 384), BF),
        pltpu.VMEM((2, 16, 14, 8, 384), BF),
        pltpu.VMEM((3, 1792, 128), F32),
        pltpu.VMEM((896, 512), BF),
        pltpu.VMEM((4, 448, 512), BF),
        pltpu.VMEM((4, 448, 512), BF),
        pltpu.VMEM((4, 448, 512), BF),
        pltpu.VMEM((4, 448, 512), BF),
        pltpu.VMEM((4, 448, 512), F32),
        pltpu.VMEM((512, 512), BF),
        pltpu.VMEM((512, 512), BF),
        pltpu.VMEM((14, 32, 8, 384), BF),
        pltpu.VMEM((14, 16, 8, 384), BF),
        pltpu.VMEM((4, 2, 14, 56, 128), BF),
        pltpu.VMEM((512, 512), F32),
        pltpu.VMEM((512, 512), F32),
        pltpu.VMEM((448, 896), BF),
        pltpu.VMEM((448, 256), BF),
        pltpu.VMEM((8, 96, 128), BF),
        pltpu.VMEM((8, 96, 128), BF),
        pltpu.VMEM((96, 128), F32),
        pltpu.VMEM((96, 128), F32),
        pltpu.VMEM((96, 128), F32),
        pltpu.VMEM((96, 128), F32),
        pltpu.VMEM((4, 96, 128), BF),
        pltpu.VMEM((8, 4, 96, 128), BF),
        pltpu.VMEM((2, 256, 448), BF),
        pltpu.VMEM((448, 896), BF),
        pltpu.VMEM((BLOCKS, 2, BLOCK_W, BLOCK_W), BF),
        pltpu.VMEM((BLOCKS, 2, BLOCK_W, BLOCK_W), BF),
        dma((2,)), dma, dma((28,)), dma, dma((28,)), dma, dma((2,)), dma, dma((14,)),
        dma, dma((14,)), dma, dma, dma((14,)), dma,
        dma, dma, dma, dma, dma, dma, dma, dma, dma, dma, dma((4,)),
    ]
    return pl.pallas_call(
        body,
        out_shape=(
            jax.ShapeDtypeStruct((28, 2, 56, 768), BF),
            jax.ShapeDtypeStruct((BLOCKS, 2, BLOCK_W, BLOCK_W), F32),
            jax.ShapeDtypeStruct((BLOCKS, 2, BLOCK_W, BLOCK_W), F32),
        ),
        in_specs=[anyspace] * 6,
        out_specs=(anyspace, vmem, vmem),
        scratch_shapes=scratch,
        compiler_params=pltpu.CompilerParams(
            collective_id=0, has_side_effects=True, vmem_limit_bytes=67043328
        ),
        name="spectral_step",
    )(fields, cotangent, inner, outer, *tables())


def local(fields, cotangent, inner_weight, outer_weight):
    field_gradient, inner_gradient, outer_gradient = step(
        fields.reshape(28, 2, 56, 768),
        cotangent.reshape(28, 2, 56, 768),
        inner_weight,
        outer_weight,
    )
    return field_gradient.reshape(fields.shape), inner_gradient, outer_gradient


def solution(mesh):
    return jax.shard_map(
        local,
        mesh=mesh,
        in_specs=(P("lat", "lon", None), P("lat", "lon", None), P(), P()),
        out_specs=(P("lat", "lon", None), P(), P()),
        check_vma=False,
    )
```
